512 devices in a mesh: req: 32 (over z, core), tensor: 16 (over y, x).
Axes of the slice: x: 4, y: 4, z: 16, core: 2. Of those that a mesh axis runs over, the one named last changes fastest.
Arguments:
- text: bfloat16 [12288, 4096], P('req', 'tensor'), may hold values from -6 to 6
- patches: bfloat16 [1024, 6, 6, 4096], P('req', None, None, 'tensor'), may hold values from -6 to 6
- grids: int32 [1024, 2], replicated, may hold values from 2 to 6, as said below
- image_request: int32 [1024], replicated, may hold values from 0 to 31, as said below
- slot_start: int32 [1024], replicated, may hold values from 1 to 375, as said below
- vis_gain: bfloat16 [4096], P('tensor'), may hold values from 0.099609375 to 1.8984375
- dec_gain: bfloat16 [4096], replicated, may hold values from 0.099609375 to 1.8984375
- w_qkv: bfloat16 [4096, 3, 2048], P(None, None, 'tensor'), may hold values from -0.09375 to 0.09375
- w_out: bfloat16 [2048, 4096], P('tensor'), may hold values from -0.125 to 0.125
Outputs:
- layer_out: bfloat16 [12288, 4096], P('req', 'tensor')
The draws below stay inside these ranges and needn't reach their ends.
Inputs may be any that keep to these rules, and one draw needn't show every extreme that they name: `grids`: heights and widths are even; some image has a 6 x 6 grid and some a 2 x 2 grid. `image_request`: the images of one index of req go to distinct requests, one to each. `slot_start`: the regions of 9 positions of the images of one request don't intersect and lie within the prompt; position 0 of every prompt lies outside them.
All inputs are finite; a program needn't handle non-finite values.
Results may differ from the reference program's by a relative error of at most 0.011.
Values may be sent and summed in bfloat16 or wider, within the bound.
A program may use at most 64 MiB of HBM per device.

```python
import jax
import jax.numpy as jnp
from jax import lax

D = 4096
HEADS = 16
HD = 128
G = 6
REGION = 9
IMG_DEV = 32
L = 384
IMAGES = 1024
TOKENS = 12288
N_REQ = 32
N_TENSOR = 16


def shared_layout(key):
    offsets = jax.random.permutation(jax.random.fold_in(key, 11), N_REQ)
    index = jnp.arange(IMAGES, dtype=jnp.int32)
    device = index // IMG_DEV
    within = index % IMG_DEV
    request = (device + offsets[within]) % N_REQ
    base = jax.random.randint(jax.random.fold_in(key, 12), (N_REQ,), 1, L - IMG_DEV * REGION + 1)
    base = base.at[0].set(L - IMG_DEV * REGION).at[1].set(1)
    start = base[request] + within * REGION
    return (request.astype(jnp.int32), start.astype(jnp.int32))


def draw_image_request(key, part):
    return shared_layout(key)[0]


def draw_slot_start(key, part):
    return shared_layout(key)[1]


def draw_grids(key, part):
    low = max(1, G // 4)
    sides = 2 * jax.random.randint(jax.random.fold_in(key, 13), (IMAGES, 2), low, G // 2 + 1)
    sides = sides.at[0].set(G).at[1].set(2)
    return sides.astype(jnp.int32)


def block_levels(key, shape, cuts, low, largest):
    def one(dim, blocks):
        steps = jax.random.uniform(jax.random.fold_in(jax.random.fold_in(key, 6), dim), (blocks,), jnp.float32, low / len(cuts), largest / len(cuts))
        return jnp.repeat(jnp.exp(steps), shape[dim] // blocks).reshape((-1,) + (1,) * (len(shape) - dim - 1))

    level = one(*cuts[0])
    for cut in cuts[1:]:
        level = level * one(*cut)
    return level


def noise(rng, dims, scale, limit, shards=(), kind=jnp.bfloat16):
    values = scale * jax.random.normal(rng, dims, jnp.float32)
    if shards:
        values = values * block_levels(rng, dims, shards, -0.22, 0.18)
    return jnp.clip(values, -limit, limit).astype(kind)


def setup_inputs(seed: int = 0) -> dict:
    streams_of = jax.random.split(jax.random.key(seed), 10)
    return {
        "text": noise(streams_of[0], (TOKENS, D), 1.0, 6.0, ((0, 32), (1, 16))),
        "patches": noise(streams_of[1], (IMAGES, G, G, D), 1.0, 6.0, ((0, 32), (3, 16))),
        "grids": draw_grids(jax.random.fold_in(streams_of[9], 71), 0),
        "image_request": draw_image_request(jax.random.fold_in(streams_of[9], 71), 0),
        "slot_start": draw_slot_start(jax.random.fold_in(streams_of[9], 71), 0),
        "vis_gain": jnp.clip(1.0 + 0.18 * jax.random.normal(streams_of[5], (D,), jnp.float32), 0.099609375, 1.8984375).astype(jnp.bfloat16),
        "dec_gain": jnp.clip(1.0 + 0.18 * jax.random.normal(streams_of[6], (D,), jnp.float32), 0.099609375, 1.8984375).astype(jnp.bfloat16),
        "w_qkv": noise(streams_of[7], (D, 3, HEADS * HD), D ** -0.5, 0.09375, ((2, 16),)),
        "w_out": noise(streams_of[8], (HEADS * HD, D), (HEADS * HD) ** -0.5, 0.125, ((0, 16),)),
    }


def merge_one(block):
    half = G // 2
    f = block.astype(jnp.float32).reshape(half, 2, half, 2, D).mean(axis=(1, 3)).reshape(REGION, D)
    return f

def reference(text, patches, grids, image_request, slot_start, vis_gain, dec_gain, w_qkv, w_out):
    half = G // 2
    gain_v = vis_gain.astype(jnp.float32)

    def merge_norm(block):
        f = merge_one(block)
        ms = lax.optimization_barrier(jnp.mean(f * f, axis=-1, keepdims=True))
        return (f * lax.rsqrt(ms + 1e-05) * gain_v).astype(jnp.bfloat16)
    merged = lax.map(merge_norm, patches)
    cells = jnp.arange(REGION, dtype=jnp.int32)
    row_i = cells // half
    col_j = cells % half
    height = grids[:, 0][:, None] // 2
    width = grids[:, 1][:, None] // 2
    valid = (row_i[None, :] < height) & (col_j[None, :] < width)
    base = image_request[:, None] * L + slot_start[:, None]
    pos = jnp.where(valid, base + row_i[None, :] * width + col_j[None, :], TOKENS).astype(jnp.int32)
    rpos = (base + cells[None, :]).astype(jnp.int32)
    img_rows = jnp.zeros((TOKENS, D), jnp.bfloat16).at[pos.reshape(-1)].set(merged.reshape(-1, D), mode='drop')
    is_img = jnp.zeros((TOKENS,), bool).at[pos.reshape(-1)].set(True, mode='drop')
    in_region = jnp.zeros((TOKENS,), bool).at[rpos.reshape(-1)].set(True, mode='drop')
    key_ok = ~in_region | is_img
    x_in = jnp.where(is_img[:, None], img_rows, text)
    heads_local = HEADS // N_TENSOR
    gain_d = dec_gain.astype(jnp.float32)
    w_flat = w_qkv.reshape(D, 3 * HEADS * HD)
    w_groups = w_out.reshape(N_TENSOR, heads_local * HD, D).astype(jnp.float32)
    causal = jnp.arange(L)[:, None] >= jnp.arange(L)[None, :]

    def one_prompt(item):
        rows, ok = item
        xf = rows.astype(jnp.float32)
        ms = lax.optimization_barrier(jnp.mean(xf * xf, axis=-1, keepdims=True))
        normed = (xf * lax.rsqrt(ms + 1e-05) * gain_d).astype(jnp.bfloat16)
        qkv = jnp.dot(normed, w_flat, preferred_element_type=jnp.float32).astype(jnp.bfloat16)
        qkv = qkv.reshape(L, 3, HEADS, HD).astype(jnp.float32)
        scores = jnp.einsum('qhd,khd->hqk', qkv[:, 0], qkv[:, 1]) / jnp.sqrt(jnp.float32(HD))
        mask = causal & ok[None, :]
        scores = jnp.where(mask[None], scores, jnp.float32(-1e+30))
        top = lax.optimization_barrier(jnp.max(scores, axis=-1, keepdims=True))
        ex = jnp.exp(scores - top)
        probs = (ex / lax.optimization_barrier(jnp.sum(ex, axis=-1, keepdims=True))).astype(jnp.bfloat16)
        context = jnp.einsum('hqk,khd->qhd', probs.astype(jnp.float32), qkv[:, 2]).astype(jnp.bfloat16)
        context = context.reshape(L, N_TENSOR, heads_local * HD).astype(jnp.float32)
        partial_value = jnp.einsum('lta,tad->tld', context, w_groups).astype(jnp.bfloat16)
        summed = lax.optimization_barrier(jnp.sum(partial_value.astype(jnp.float32), axis=0))
        return (xf + summed).astype(jnp.bfloat16)
    out = lax.map(one_prompt, (x_in.reshape(N_REQ, L, D), key_ok.reshape(N_REQ, L)))
    return out.reshape(TOKENS, D)
```

```python
import functools

import jax
import jax.numpy as jnp
from jax import lax
from jax.experimental import pallas as pl
from jax.experimental.pallas import tpu as pltpu
from jax.sharding import PartitionSpec as P

D = 4096
HD = 128
L = 384
W = 256
NR = 32
NT = 16
IMG = 32
CELLS = 9
SLOT = 24
ROWS = L + 8
EPS = 1e-05
MESH = pl.DeviceIdType.MESH
F32 = jnp.float32
BF16 = jnp.bfloat16


def iota(shape, dim):
    return lax.broadcasted_iota(jnp.int32, shape, dim)


def dot(a, b):
    return lax.dot_general(a, b, (((1,), (0,)), ((), ())), preferred_element_type=F32)


def dot_nt(a, b):
    return lax.dot_general(a, b, (((1,), (1,)), ((), ())), preferred_element_type=F32)


def kernel(
    text_h, patch_h, grid_r, req_r, slot_r, gv_r, gd_r, wqkv_h, wout_h, out_r,
    text_v, patch_v, w_v, wcol, stage_f, stage, recv, recv_f, place, rcat, xraw_v, xfull, cfull,
    acc, oacc, loc_sem, w_send, w_recv, a_send, a_recv, x_send, x_recv, c_send, c_recv,
):
    me_r = lax.axis_index("req")
    me_t = lax.axis_index("tensor")

    load_p = pltpu.make_async_copy(patch_h, patch_v, loc_sem.at[0])
    load_t = pltpu.make_async_copy(text_h, text_v, loc_sem.at[1])
    load_w = [
        pltpu.make_async_copy(wqkv_h.at[j], w_v.at[:, pl.ds(j * HD, HD)], loc_sem.at[2 + j])
        for j in range(3)
    ]
    own_cols = pl.ds(pl.multiple_of(me_t * W, W), W)
    load_o = pltpu.make_async_copy(wout_h.at[:, own_cols], wcol.at[me_t], loc_sem.at[5])
    load_p.start()
    barrier = pltpu.get_barrier_semaphore()

    def greet_r(d, _):
        pl.semaphore_signal(
            barrier, inc=1, device_id={"req": lax.rem(me_r + d, NR)}, device_id_type=MESH
        )
        return _

    def greet_t(d, _):
        pl.semaphore_signal(
            barrier, inc=1, device_id={"tensor": lax.rem(me_t + d, NT)}, device_id_type=MESH
        )
        return _

    lax.fori_loop(1, NR, greet_r, 0)
    lax.fori_loop(1, NT, greet_t, 0)
    load_t.start()
    for copy in load_w:
        copy.start()
    load_o.start()

    lane = iota((1, NR * IMG), 1)
    req = req_r[...]
    own_sel = (iota((IMG, NR * IMG), 1) == me_r * IMG + iota((IMG, NR * IMG), 0)).astype(BF16)
    req8 = jnp.broadcast_to(req.astype(F32), (8, NR * IMG)).astype(BF16)
    own = dot_nt(req8, own_sel)[0:1, :]
    onehot = (iota((NR, IMG), 0).astype(F32) == own).astype(BF16)
    load_p.wait()
    stage_f[...] = jnp.zeros_like(stage_f)
    for c in range(CELLS):
        i, j = 2 * (c // 3), 2 * (c % 3)
        total = (
            patch_v[i, j].astype(F32) + patch_v[i, j + 1].astype(F32)
            + patch_v[i + 1, j].astype(F32) + patch_v[i + 1, j + 1].astype(F32)
        )
        sent = dot(onehot, (total * 0.25).astype(BF16))
        stage_f[pl.ds(c, NR, stride=SLOT), :] = sent[:, :HD]
        stage_f[pl.ds(CELLS + c, NR, stride=SLOT), :] = sent[:, HD:]
    stage[...] = stage_f[...].astype(BF16).reshape(NR, SLOT, HD)

    pl.semaphore_wait(barrier, NR - 1 + NT - 1)

    def a_copy(d):
        to = lax.rem(me_r + d, NR)
        return pltpu.make_async_remote_copy(
            src_ref=stage.at[to], dst_ref=recv.at[me_r], send_sem=a_send.at[d],
            recv_sem=a_recv.at[me_r], device_id={"req": to}, device_id_type=MESH,
        )

    def a_wait(d):
        frm = lax.rem(me_r + d, NR)
        pltpu.make_async_remote_copy(
            src_ref=stage.at[frm], dst_ref=recv.at[frm], send_sem=a_send.at[d],
            recv_sem=a_recv.at[frm], device_id={"req": frm}, device_id_type=MESH,
        ).wait_recv()

    def w_copy(d):
        to = lax.rem(me_t + d, NT)
        cols = pl.ds(pl.multiple_of(to * W, W), W)
        return pltpu.make_async_remote_copy(
            src_ref=wout_h.at[:, cols], dst_ref=wcol.at[me_t], send_sem=w_send.at[d],
            recv_sem=w_recv.at[me_t], device_id={"tensor": to}, device_id_type=MESH,
        )

    def t_copy(buf, send, rec, d):
        to = lax.rem(me_t + d, NT)
        return pltpu.make_async_remote_copy(
            src_ref=buf.at[me_t], dst_ref=buf.at[me_t], send_sem=send.at[d],
            recv_sem=rec.at[me_t], device_id={"tensor": to}, device_id_type=MESH,
        )

    def t_wait(buf, send, rec, d):
        frm = lax.rem(me_t + d, NT)
        pltpu.make_async_remote_copy(
            src_ref=buf.at[frm], dst_ref=buf.at[frm], send_sem=send.at[d],
            recv_sem=rec.at[frm], device_id={"tensor": frm}, device_id_type=MESH,
        ).wait_recv()
        return frm

    def loop(lo, hi, f):
        def step(d, _):
            f(d)
            return _
        lax.fori_loop(lo, hi, step, 0)

    loop(1, NR, lambda d: a_copy(d).start())
    loop(1, NT, lambda d: w_copy(d).start())
    recv[me_r] = stage[me_r]

    row = iota((8, NR * IMG), 0)
    start = jnp.broadcast_to(slot_r[...], (8, NR * IMG))
    half_h = jnp.broadcast_to(grid_r[0:1, :], (8, NR * IMG)) // 2
    half_w = jnp.broadcast_to(grid_r[1:2, :], (8, NR * IMG)) // 2
    facts = jnp.where(
        row == 0, start // 16, jnp.where(row == 1, start % 16, jnp.where(row == 2, half_h, half_w))
    )
    facts = jnp.where(jnp.broadcast_to(req, (8, NR * IMG)) == me_r, facts, 0).astype(F32).astype(BF16)
    seg = (iota((NR, NR * IMG), 1) // IMG == iota((NR, NR * IMG), 0)).astype(BF16)
    by_lane = dot_nt(facts, seg)
    by_row = dot_nt(seg, facts)
    start_l = by_lane[0:1, :] * 16.0 + by_lane[1:2, :]
    hh_l, hw_l = by_lane[2:3, :], by_lane[3:4, :]
    position = iota((L, NR), 0).astype(F32)
    hits = jnp.zeros((L, NR), F32)
    for c in range(CELLS):
        i, j = float(c // 3), float(c % 3)
        pos = jnp.where((hh_l > i) & (hw_l > j), start_l + i * hw_l + j, -1.0)
        hit = (position == pos).astype(F32)
        hits = hits + hit
        place[:, c * NR:(c + 1) * NR] = hit.astype(BF16)
    is_img = jnp.sum(hits, axis=1, keepdims=True) > 0.5
    start_c = by_row[:, 0:1] * 16.0 + by_row[:, 1:2]
    filled_c = by_row[:, 2:3] * by_row[:, 3:4]
    off = iota((NR, L), 1).astype(F32) - start_c
    img_l = jnp.max(((off >= 0.0) & (off < filled_c)).astype(F32), axis=0, keepdims=True)
    bad_l = jnp.max(((off >= filled_c) & (off < float(CELLS))).astype(F32), axis=0, keepdims=True)

    load_t.wait()
    gv = gv_r[...].astype(F32)
    gd = gd_r[:, own_cols].astype(F32)

    loop(1, NR, a_wait)
    recv_f[...] = recv[...].reshape(NR * SLOT, HD).astype(F32)
    for c in range(CELLS):
        rcat[c * NR:(c + 1) * NR, :HD] = recv_f[pl.ds(c, NR, stride=SLOT), :].astype(BF16)
        rcat[c * NR:(c + 1) * NR, HD:] = recv_f[pl.ds(CELLS + c, NR, stride=SLOT), :].astype(BF16)
    img = dot(place[...], rcat[...])
    xraw = jnp.where(is_img, img * gv, text_v[...].astype(F32))
    xraw_v[...] = xraw
    xfull[me_t, :L, :] = (xraw * gd).astype(BF16)
    ones = jnp.ones((8, W), BF16)
    s_img = dot_nt(ones, (img * img).astype(BF16))
    s_row = dot_nt(ones, (xraw * xraw).astype(BF16))

    def two(s, r):
        hi = s.astype(BF16).astype(F32)
        lo = s - hi
        def wide(v):
            return jnp.concatenate([v[:, W:], jnp.zeros((8, 2 * W - L), F32)], axis=1)
        return jnp.where(
            r == 0, hi[:, :W], jnp.where(r == 1, wide(hi), jnp.where(r == 2, lo[:, :W], wide(lo)))
        )

    r8 = iota((8, W), 0)
    xfull[me_t, L:, :] = jnp.where(r8 < 4, two(s_img, r8), two(s_row, r8 - 4)).astype(BF16)

    loop(1, NT, lambda d: t_copy(xfull, x_send, x_recv, d).start())
    for copy in load_w:
        copy.wait()
    load_o.wait()

    def project(t):
        rows = pl.ds(pl.multiple_of(t * W, W), W)
        return dot(xfull[t, :L, :], w_v[rows, :])

    acc[...] = project(me_t)

    def gather_x(d, sums):
        t = t_wait(xfull, x_send, x_recv, d)
        acc[...] += project(t)
        return sums + xfull[t, L:, :].astype(F32)

    sums = lax.fori_loop(1, NT, gather_x, xfull[me_t, L:, :].astype(F32))

    def whole(r):
        return jnp.concatenate(
            [sums[r:r + 1, :] + sums[r + 2:r + 3, :],
             sums[r + 1:r + 2, :L - W] + sums[r + 3:r + 4, :L - W]], axis=1
        )

    s1, s2 = whole(0), whole(4)
    rv = jnp.where(img_l > 0.5, lax.rsqrt(s1 / D + EPS), 1.0)
    rd = lax.rsqrt(rv * rv * s2 / D + EPS)
    r8l = iota((8, L), 0)
    cols = jnp.transpose(jnp.where(r8l == 0, rv * rd, rv))
    scale_c, rv_c = cols[:, 0:1], cols[:, 1:2]
    qkv = (acc[...] * scale_c).astype(BF16)
    scores = dot_nt(qkv[:, :HD], qkv[:, HD:2 * HD]) * (HD ** -0.5)
    keep = (iota((L, L), 0) >= iota((L, L), 1)) & (bad_l < 0.5)
    scores = jnp.where(keep, scores, -1e30)
    top = jnp.max(scores, axis=-1, keepdims=True)
    expo = jnp.exp(scores - top)
    probs = (expo / jnp.sum(expo, axis=-1, keepdims=True)).astype(BF16)
    cfull[me_t] = dot(probs, qkv[:, 2 * HD:]).astype(BF16)
    loop(1, NT, lambda d: t_copy(cfull, c_send, c_recv, d).start())
    oacc[...] = dot(cfull[me_t], wcol[me_t])

    def gather_c(d):
        t_wait(wcol, w_send, w_recv, d)
        t = t_wait(cfull, c_send, c_recv, d)
        oacc[...] += dot(cfull[t], wcol[t])

    loop(1, NT, gather_c)
    x_in = (xraw_v[...] * rv_c).astype(BF16).astype(F32)
    out_r[...] = (x_in + oacc[...]).astype(BF16)

    loop(1, NR, lambda d: a_copy(d).wait_send())
    loop(1, NT, lambda d: w_copy(d).wait_send())
    loop(1, NT, lambda d: t_copy(xfull, x_send, x_recv, d).wait_send())
    loop(1, NT, lambda d: t_copy(cfull, c_send, c_recv, d).wait_send())


def body(text, patches, grids, image_request, slot_start, vis_gain, dec_gain, w_qkv, w_out):
    vmem = pl.BlockSpec(memory_space=pltpu.VMEM)
    hbm = pl.BlockSpec(memory_space=pl.ANY)
    dma = pltpu.SemaphoreType.DMA
    return pl.pallas_call(
        kernel,
        out_shape=jax.ShapeDtypeStruct((L, W), BF16),
        in_specs=[hbm, hbm, vmem, vmem, vmem, vmem, vmem, hbm, hbm],
        out_specs=vmem,
        scratch_shapes=[
            pltpu.VMEM((L, W), BF16),
            pltpu.VMEM((6, 6, IMG, W), BF16),
            pltpu.VMEM((D, 3 * HD), BF16),
            pltpu.VMEM((NT, HD, W), BF16),
            pltpu.VMEM((NR * SLOT, HD), F32),
            pltpu.VMEM((NR, SLOT, HD), BF16),
            pltpu.VMEM((NR, SLOT, HD), BF16),
            pltpu.VMEM((NR * SLOT, HD), F32),
            pltpu.VMEM((L, CELLS * NR), BF16),
            pltpu.VMEM((CELLS * NR, W), BF16),
            pltpu.VMEM((L, W), F32),
            pltpu.VMEM((NT, ROWS, W), BF16),
            pltpu.VMEM((NT, L, HD), BF16),
            pltpu.VMEM((L, 3 * HD), F32),
            pltpu.VMEM((L, W), F32),
            dma((6,)), dma((NT,)), dma((NT,)), dma((NR,)), dma((NR,)),
            dma((NT,)), dma((NT,)), dma((NT,)), dma((NT,)),
        ],
        compiler_params=pltpu.CompilerParams(
            collective_id=0, has_side_effects=True, vmem_limit_bytes=48 * 2**20
        ),
    )(
        text,
        patches.transpose(1, 2, 0, 3),
        grids.T,
        image_request.reshape(1, -1),
        slot_start.reshape(1, -1),
        vis_gain.reshape(1, -1),
        dec_gain.reshape(1, -1),
        w_qkv.transpose(1, 0, 2),
        w_out,
    )


def solution(mesh):
    in_specs = (
        P("req", "tensor"),
        P("req", None, None, "tensor"),
        P(),
        P(),
        P(),
        P("tensor"),
        P(),
        P(None, None, "tensor"),
        P("tensor", None),
    )
    return jax.shard_map(
        body, mesh=mesh, in_specs=in_specs, out_specs=P("req", "tensor"), check_vma=False
    )
```

```python
import functools

import jax
import jax.numpy as jnp
from jax import lax
from jax.experimental import pallas as pl
from jax.experimental.pallas import tpu as pltpu
from jax.sharding import PartitionSpec as P

D = 4096
HD = 128
L = 384
W = 256
NR = 32
NT = 16
IMG = 32
CELLS = 9
SLOT = 24
ROWS = L + 8
EPS = 1e-05
MESH = pl.DeviceIdType.MESH
F32 = jnp.float32
BF16 = jnp.bfloat16

UP_A, DN_A, UP_B, DN_B = (1, 0), (-1, 0), (0, 1), (0, -1)
BOTH_B = (UP_B, DN_B)
AHEAD = (
    (UP_A, DN_A, UP_B, DN_B),
    (
        (
            (-1, 0, 0, (UP_A,) + BOTH_B), (1, 0, 0, BOTH_B), (0, -1, 0, (UP_B,)), (0, 1, 0, ()),
            (1, 0, 1, (DN_A,) + BOTH_B), (-1, 0, 1, BOTH_B), (0, 1, 1, (DN_B,)), (0, -1, 1, ()),
        ),
        (
            (2, 0, 0, BOTH_B), (2, 0, 1, BOTH_B),
            (-1, -1, 0, (UP_B,)), (1, -1, 0, (UP_B,)), (-1, 1, 0, ()), (1, 1, 0, ()),
            (-1, 1, 1, (DN_B,)), (1, 1, 1, (DN_B,)), (-1, -1, 1, ()), (1, -1, 1, ()),
            (0, 2, 0, ()), (0, 2, 1, ()),
        ),
        (
            (2, -1, 0, (UP_B,)), (2, 1, 0, ()), (2, 1, 1, (DN_B,)), (2, -1, 1, ()),
            (-1, 2, 0, ()), (-1, 2, 1, ()), (1, 2, 0, ()), (1, 2, 1, ()),
        ),
        ((2, 2, 0, ()), (2, 2, 1, ())),
    ),
)
SENDS = 30


def iota(shape, dim):
    return lax.broadcasted_iota(jnp.int32, shape, dim)


def dot(a, b):
    return lax.dot_general(a, b, (((1,), (0,)), ((), ())), preferred_element_type=F32)


def dot_nt(a, b):
    return lax.dot_general(a, b, (((1,), (1,)), ((), ())), preferred_element_type=F32)


def kernel(
    text_h, patch_h, grid_r, req_r, slot_r, gv_r, gd_r, wqkv_h, wout_h, out_r,
    text_v, patch_v, w_v, wcol, stage_f, stage, recv, recv_f, place, rcat, xraw_v, xfull, cfull,
    acc, oacc, stat, loc_sem, w_send, w_recv, a_send, a_recv, x_send, x_recv, c_send, c_recv,
):
    me_r = lax.axis_index("req")
    me_t = lax.axis_index("tensor")

    load_p = pltpu.make_async_copy(patch_h, patch_v, loc_sem.at[0])
    load_t = pltpu.make_async_copy(text_h, text_v, loc_sem.at[1])
    load_w = [
        pltpu.make_async_copy(wqkv_h.at[j], w_v.at[:, pl.ds(j * HD, HD)], loc_sem.at[2 + j])
        for j in range(3)
    ]
    own_cols = pl.ds(pl.multiple_of(me_t * W, W), W)
    load_o = pltpu.make_async_copy(wout_h.at[:, own_cols], wcol.at[me_t], loc_sem.at[5])
    load_p.start()
    barrier = pltpu.get_barrier_semaphore()

    def greet_r(d, _):
        pl.semaphore_signal(
            barrier, inc=1, device_id={"req": lax.rem(me_r + d, NR)}, device_id_type=MESH
        )
        return _

    def greet_t(d, _):
        pl.semaphore_signal(
            barrier, inc=1, device_id={"tensor": lax.rem(me_t + d, NT)}, device_id_type=MESH
        )
        return _

    lax.fori_loop(1, NR, greet_r, 0)
    lax.fori_loop(1, NT, greet_t, 0)
    load_t.start()
    for copy in load_w:
        copy.start()
    load_o.start()

    lane = iota((1, NR * IMG), 1)
    req = req_r[...]
    own_sel = (iota((IMG, NR * IMG), 1) == me_r * IMG + iota((IMG, NR * IMG), 0)).astype(BF16)
    req8 = jnp.broadcast_to(req.astype(F32), (8, NR * IMG)).astype(BF16)
    own = dot_nt(req8, own_sel)[0:1, :]
    onehot = (iota((NR, IMG), 0).astype(F32) == own).astype(BF16)
    load_p.wait()
    stage_f[...] = jnp.zeros_like(stage_f)
    for c in range(CELLS):
        i, j = 2 * (c // 3), 2 * (c % 3)
        total = (
            patch_v[i, j].astype(F32) + patch_v[i, j + 1].astype(F32)
            + patch_v[i + 1, j].astype(F32) + patch_v[i + 1, j + 1].astype(F32)
        )
        sent = dot(onehot, (total * 0.25).astype(BF16))
        stage_f[pl.ds(c, NR, stride=SLOT), :] = sent[:, :HD]
        stage_f[pl.ds(CELLS + c, NR, stride=SLOT), :] = sent[:, HD:]
    stage[...] = stage_f[...].astype(BF16).reshape(NR, SLOT, HD)

    pl.semaphore_wait(barrier, NR - 1 + NT - 1)

    def a_copy(d):
        to = lax.rem(me_r + d, NR)
        return pltpu.make_async_remote_copy(
            src_ref=stage.at[to], dst_ref=recv.at[me_r], send_sem=a_send.at[d],
            recv_sem=a_recv.at[me_r], device_id={"req": to}, device_id_type=MESH,
        )

    def a_wait(d):
        frm = lax.rem(me_r + d, NR)
        pltpu.make_async_remote_copy(
            src_ref=stage.at[frm], dst_ref=recv.at[frm], send_sem=a_send.at[d],
            recv_sem=a_recv.at[frm], device_id={"req": frm}, device_id_type=MESH,
        ).wait_recv()

    def w_copy(d):
        to = lax.rem(me_t + d, NT)
        cols = pl.ds(pl.multiple_of(to * W, W), W)
        return pltpu.make_async_remote_copy(
            src_ref=wout_h.at[:, cols], dst_ref=wcol.at[me_t], send_sem=w_send.at[d],
            recv_sem=w_recv.at[me_t], device_id={"tensor": to}, device_id_type=MESH,
        )

    def w_wait(d):
        frm = lax.rem(me_t + d, NT)
        pltpu.make_async_remote_copy(
            src_ref=wcol.at[frm], dst_ref=wcol.at[frm], send_sem=w_send.at[d],
            recv_sem=w_recv.at[frm], device_id={"tensor": frm}, device_id_type=MESH,
        ).wait_recv()

    core = lax.rem(me_r, 2)
    tx, ty = lax.rem(me_t, 4), me_t // 4
    pa, pb = tx + core * (ty - tx), ty + core * (tx - ty)
    sa, sb = 1 + 3 * core, 4 - 3 * core

    def at(da, db):
        return lax.rem(pa + da + 4, 4) * sa + lax.rem(pb + db + 4, 4) * sb

    def hop(buf, cut, send, rec, da, db, h, ka, kb, k):
        t, to = at(da, db), at(ka, kb)
        rows = pl.ds(0, cut) if h == 0 else pl.ds(cut, buf.shape[1] - cut)
        return pltpu.make_async_remote_copy(
            src_ref=buf.at[t, rows], dst_ref=buf.at[t, rows], send_sem=send.at[k],
            recv_sem=rec.at[t, h], device_id={"tensor": to}, device_id_type=MESH,
        )

    def gather(buf, cut, send, rec, use):
        sent = []

        def push(da, db, h, *to):
            for ka, kb in to:
                copy = hop(buf, cut, send, rec, da, db, h, ka, kb, len(sent))
                copy.start()
                sent.append(copy)

        for h in range(2):
            push(0, 0, h, *AHEAD[0])
        use(at(0, 0))
        for group in AHEAD[1]:
            for da, db, h, to in group:
                hop(buf, cut, send, rec, da, db, h, 0, 1, 0).wait_recv()
                push(da, db, h, *to)
            for da, db in sorted({(g[0], g[1]) for g in group if g[2] == 1}):
                use(at(da, db))
        return sent

    def loop(lo, hi, f):
        def step(d, _):
            f(d)
            return _
        lax.fori_loop(lo, hi, step, 0)

    loop(1, NR, lambda d: a_copy(d).start())
    loop(1, NT, lambda d: w_copy(d).start())
    recv[me_r] = stage[me_r]

    row = iota((8, NR * IMG), 0)
    start = jnp.broadcast_to(slot_r[...], (8, NR * IMG))
    half_h = jnp.broadcast_to(grid_r[0:1, :], (8, NR * IMG)) // 2
    half_w = jnp.broadcast_to(grid_r[1:2, :], (8, NR * IMG)) // 2
    facts = jnp.where(
        row == 0, start // 16, jnp.where(row == 1, start % 16, jnp.where(row == 2, half_h, half_w))
    )
    facts = jnp.where(jnp.broadcast_to(req, (8, NR * IMG)) == me_r, facts, 0).astype(F32).astype(BF16)
    seg = (iota((NR, NR * IMG), 1) // IMG == iota((NR, NR * IMG), 0)).astype(BF16)
    by_lane = dot_nt(facts, seg)
    by_row = dot_nt(seg, facts)
    start_l = by_lane[0:1, :] * 16.0 + by_lane[1:2, :]
    hh_l, hw_l = by_lane[2:3, :], by_lane[3:4, :]
    position = iota((L, NR), 0).astype(F32)
    hits = jnp.zeros((L, NR), F32)
    for c in range(CELLS):
        i, j = float(c // 3), float(c % 3)
        pos = jnp.where((hh_l > i) & (hw_l > j), start_l + i * hw_l + j, -1.0)
        hit = (position == pos).astype(F32)
        hits = hits + hit
        place[:, c * NR:(c + 1) * NR] = hit.astype(BF16)
    is_img = jnp.sum(hits, axis=1, keepdims=True) > 0.5
    start_c = by_row[:, 0:1] * 16.0 + by_row[:, 1:2]
    filled_c = by_row[:, 2:3] * by_row[:, 3:4]
    off = iota((NR, L), 1).astype(F32) - start_c
    img_l = jnp.max(((off >= 0.0) & (off < filled_c)).astype(F32), axis=0, keepdims=True)
    bad_l = jnp.max(((off >= filled_c) & (off < float(CELLS))).astype(F32), axis=0, keepdims=True)

    load_t.wait()
    gv = gv_r[...].astype(F32)
    gd = gd_r[:, own_cols].astype(F32)

    loop(1, NR, a_wait)
    recv_f[...] = recv[...].reshape(NR * SLOT, HD).astype(F32)
    for c in range(CELLS):
        rcat[c * NR:(c + 1) * NR, :HD] = recv_f[pl.ds(c, NR, stride=SLOT), :].astype(BF16)
        rcat[c * NR:(c + 1) * NR, HD:] = recv_f[pl.ds(CELLS + c, NR, stride=SLOT), :].astype(BF16)
    img = dot(place[...], rcat[...])
    xraw = jnp.where(is_img, img * gv, text_v[...].astype(F32))
    xraw_v[...] = xraw
    xfull[me_t, :L, :] = (xraw * gd).astype(BF16)
    ones = jnp.ones((8, W), BF16)
    s_img = dot_nt(ones, (img * img).astype(BF16))
    s_row = dot_nt(ones, (xraw * xraw).astype(BF16))

    def two(s, r):
        hi = s.astype(BF16).astype(F32)
        lo = s - hi
        def wide(v):
            return jnp.concatenate([v[:, W:], jnp.zeros((8, 2 * W - L), F32)], axis=1)
        return jnp.where(
            r == 0, hi[:, :W], jnp.where(r == 1, wide(hi), jnp.where(r == 2, lo[:, :W], wide(lo)))
        )

    r8 = iota((8, W), 0)
    xfull[me_t, L:, :] = jnp.where(r8 < 4, two(s_img, r8), two(s_row, r8 - 4)).astype(BF16)

    for copy in load_w:
        copy.wait()
    load_o.wait()
    acc[...] = jnp.zeros_like(acc)
    stat[...] = jnp.zeros_like(stat)

    def project(t):
        rows = pl.ds(pl.multiple_of(t * W, W), W)
        acc[...] += dot(xfull[t, :L, :], w_v[rows, :])
        stat[...] += xfull[t, L:, :].astype(F32)

    x_sent = gather(xfull, 200, x_send, x_recv, project)
    sums = stat[...]

    def whole(r):
        return jnp.concatenate(
            [sums[r:r + 1, :] + sums[r + 2:r + 3, :],
             sums[r + 1:r + 2, :L - W] + sums[r + 3:r + 4, :L - W]], axis=1
        )

    s1, s2 = whole(0), whole(4)
    rv = jnp.where(img_l > 0.5, lax.rsqrt(s1 / D + EPS), 1.0)
    rd = lax.rsqrt(rv * rv * s2 / D + EPS)
    r8l = iota((8, L), 0)
    cols = jnp.transpose(jnp.where(r8l == 0, rv * rd, rv))
    scale_c, rv_c = cols[:, 0:1], cols[:, 1:2]
    qkv = (acc[...] * scale_c).astype(BF16)
    scores = dot_nt(qkv[:, :HD], qkv[:, HD:2 * HD]) * (HD ** -0.5)
    keep = (iota((L, L), 0) >= iota((L, L), 1)) & (bad_l < 0.5)
    scores = jnp.where(keep, scores, -1e30)
    top = jnp.max(scores, axis=-1, keepdims=True)
    expo = jnp.exp(scores - top)
    probs = (expo / jnp.sum(expo, axis=-1, keepdims=True)).astype(BF16)
    cfull[me_t] = dot(probs, qkv[:, 2 * HD:]).astype(BF16)
    loop(1, NT, w_wait)
    oacc[...] = jnp.zeros_like(oacc)

    def combine(t):
        oacc[...] += dot(cfull[t], wcol[t])

    c_sent = gather(cfull, L // 2, c_send, c_recv, combine)
    x_in = (xraw_v[...] * rv_c).astype(BF16).astype(F32)
    out_r[...] = (x_in + oacc[...]).astype(BF16)

    loop(1, NR, lambda d: a_copy(d).wait_send())
    loop(1, NT, lambda d: w_copy(d).wait_send())
    for copy in x_sent + c_sent:
        copy.wait_send()


def body(text, patches, grids, image_request, slot_start, vis_gain, dec_gain, w_qkv, w_out):
    vmem = pl.BlockSpec(memory_space=pltpu.VMEM)
    hbm = pl.BlockSpec(memory_space=pl.ANY)
    dma = pltpu.SemaphoreType.DMA
    return pl.pallas_call(
        kernel,
        out_shape=jax.ShapeDtypeStruct((L, W), BF16),
        in_specs=[hbm, hbm, vmem, vmem, vmem, vmem, vmem, hbm, hbm],
        out_specs=vmem,
        scratch_shapes=[
            pltpu.VMEM((L, W), BF16),
            pltpu.VMEM((6, 6, IMG, W), BF16),
            pltpu.VMEM((D, 3 * HD), BF16),
            pltpu.VMEM((NT, HD, W), BF16),
            pltpu.VMEM((NR * SLOT, HD), F32),
            pltpu.VMEM((NR, SLOT, HD), BF16),
            pltpu.VMEM((NR, SLOT, HD), BF16),
            pltpu.VMEM((NR * SLOT, HD), F32),
            pltpu.VMEM((L, CELLS * NR), BF16),
            pltpu.VMEM((CELLS * NR, W), BF16),
            pltpu.VMEM((L, W), F32),
            pltpu.VMEM((NT, ROWS, W), BF16),
            pltpu.VMEM((NT, L, HD), BF16),
            pltpu.VMEM((L, 3 * HD), F32),
            pltpu.VMEM((L, W), F32),
            pltpu.VMEM((8, W), F32),
            dma((6,)), dma((NT,)), dma((NT,)), dma((NR,)), dma((NR,)),
            dma((SENDS,)), dma((NT, 2)), dma((SENDS,)), dma((NT, 2)),
        ],
        compiler_params=pltpu.CompilerParams(
            collective_id=0, has_side_effects=True, vmem_limit_bytes=62 * 2**20
        ),
    )(
        text,
        patches.transpose(1, 2, 0, 3),
        grids.T,
        image_request.reshape(1, -1),
        slot_start.reshape(1, -1),
        vis_gain.reshape(1, -1),
        dec_gain.reshape(1, -1),
        w_qkv.transpose(1, 0, 2),
        w_out,
    )


def solution(mesh):
    in_specs = (
        P("req", "tensor"),
        P("req", None, None, "tensor"),
        P(),
        P(),
        P(),
        P("tensor"),
        P(),
        P(None, None, "tensor"),
        P("tensor", None),
    )
    return jax.shard_map(
        body, mesh=mesh, in_specs=in_specs, out_specs=P("req", "tensor"), check_vma=False
    )
```

```python
import jax
import jax.numpy as jnp
from jax import lax
from jax.experimental import pallas as pl
from jax.experimental.pallas import tpu as pltpu
from jax.sharding import PartitionSpec as P

D = 4096
HD = 128
L = 384
W = 256
NR = 32
NZ = 16
NT = 16
IMG = 32
CELLS = 9
TEXT = L - NR * CELLS
PACK = 40
GROUP = 72
EPS = 1e-05
MESH = pl.DeviceIdType.MESH
F32 = jnp.float32
BF16 = jnp.bfloat16
X_BLOCKS = ((0, 96), (96, 72), (168, 72), (240, 72), (312, 80))
X_START = (0.0, 2.5, 4.0, 5.5, 7.0)
C_BLOCKS = ((0, 192), (192, 192))
C_START = (0.0, 0.5)
PHASES = 5


def iota(shape, dim):
    return lax.broadcasted_iota(jnp.int32, shape, dim)


def dot(a, b):
    return lax.dot_general(a, b, (((1,), (0,)), ((), ())), preferred_element_type=F32)


def dot_nt(a, b):
    return lax.dot_general(a, b, (((1,), (1,)), ((), ())), preferred_element_type=F32)


def shift_of(e):
    return (e + 1) // 2 if e % 2 else -(e // 2)


def mirror(e):
    return e if e in (0, NZ - 1) else (e + 1 if e % 2 else e - 1)


def order(starts):
    keys = [(start + p, b, p) for b, start in enumerate(starts) for p in range(PHASES)]
    return [(b, p) for _, b, p in sorted(keys)]


def cell_of(n):
    e = (n * 3641) >> 16
    q = n - 18 * e
    s = (q >= CELLS).astype(jnp.int32)
    c = q - CELLS * s
    i = (c >= 3).astype(jnp.int32) + (c >= 6).astype(jnp.int32)
    return e, s, c.astype(F32), i.astype(F32), (c - 3 * i).astype(F32)


def place_of(start, hh, hw, c, i, j):
    valid = (i < hh) & (j < hw)
    before = jnp.minimum(i, hh) * hw + jnp.where(i < hh, jnp.minimum(j, hw), 0.0)
    return start + jnp.where(valid, i * hw + j, hh * hw + c - before), valid


def kernel(
    text_h, patch_h, grid_r, req_r, slot_r, gv_r, gd_r, wqkv_h, wout_h, out_r,
    text_v, patch_v, w_v, wcol, pool, stage_f, stage, recv, to_slot, to_pos, xraw, sq_i, sq_r,
    xfull, cfull, acc, oacc, stat, loc_sem, p_sem, w_send, w_recv, a_send, a_recv,
    x_send, x_recv, c_send, c_recv,
):
    me_r = lax.axis_index("req")
    me_t = lax.axis_index("tensor")
    core = lax.rem(me_r, 2)
    me_z = me_r // 2
    sibling = me_r + 1 - 2 * core
    tx, ty = lax.rem(me_t, 4), me_t // 4
    pa, pb = tx + core * (ty - tx), ty + core * (tx - ty)
    sa, sb = 1 + 3 * core, 4 - 3 * core

    def at(da, db):
        return lax.rem(pa + da + 4, 4) * sa + lax.rem(pb + db + 4, 4) * sb

    def z_peer(shift):
        return lax.rem(me_z + shift + NZ, NZ) * 2 + core

    half = pl.ds(pl.multiple_of(core * (HD // 2), HD // 2), HD // 2)

    def w_cols(t):
        return pl.ds(pl.multiple_of(t * W, W), W)

    load_p = pltpu.make_async_copy(patch_h, patch_v, loc_sem.at[0])
    load_t = pltpu.make_async_copy(text_h, text_v, loc_sem.at[1])
    load_w = [
        pltpu.make_async_copy(wqkv_h.at[j], w_v.at[:, pl.ds(j * HD, HD)], loc_sem.at[2 + j])
        for j in range(3)
    ]
    load_o = pltpu.make_async_copy(
        wout_h.at[half, w_cols(me_t)], wcol.at[me_t, half], loc_sem.at[5]
    )
    load_p.start()
    barrier = pltpu.get_barrier_semaphore()

    def greet(**device):
        pl.semaphore_signal(barrier, inc=1, device_id=device, device_id_type=MESH)

    for e in range(NZ - 1, 0, -1):
        greet(req=z_peer(shift_of(e)))
    greet(req=sibling)
    for d in range(1, NT):
        greet(tensor=lax.rem(me_t + d, NT))
    load_t.start()
    load_o.start()
    for copy in load_w:
        copy.start()

    req = req_r[...]
    req8 = jnp.broadcast_to(req.astype(F32), (8, NR * IMG)).astype(BF16)
    ours = (
        iota((2 * IMG, NR * IMG), 1) == me_z * 2 * IMG + iota((2 * IMG, NR * IMG), 0)
    ).astype(BF16)
    goes = dot_nt(req8, ours)[0:1, :]
    row_s = (iota((NR, 2 * IMG), 0) >= NZ).astype(jnp.int32)
    col_s = (iota((NR, 2 * IMG), 1) >= IMG).astype(jnp.int32)
    wanted = ((iota((NR, 2 * IMG), 0) - NZ * row_s) * 2 + core).astype(F32)
    pick = ((row_s == col_s) & (wanted == goes)).astype(BF16)

    load_p.wait()
    for c in range(CELLS):
        i, j = 2 * (c // 3), 2 * (c % 3)
        total = (
            patch_v[i, j].astype(F32) + patch_v[i, j + 1].astype(F32)
            + patch_v[i + 1, j].astype(F32) + patch_v[i + 1, j + 1].astype(F32)
        )
        pool[c, core] = (total * 0.25).astype(BF16)
    stage_f[...] = jnp.zeros_like(stage_f)

    pl.semaphore_wait(barrier, NZ - 1 + 1 + NT - 1)

    swap = pltpu.make_async_remote_copy(
        src_ref=pool.at[:, core], dst_ref=pool.at[:, core], send_sem=p_sem.at[0],
        recv_sem=p_sem.at[1], device_id={"req": sibling}, device_id_type=MESH,
    )
    swap.start()
    swap.wait_recv()
    for c in range(CELLS):
        sent = dot(pick, pool[c].reshape(2 * IMG, W))
        for s in range(2):
            rows = sent[s * NZ:(s + 1) * NZ]
            stage_f[pl.ds(s * CELLS + c, NZ, stride=PACK), :] = rows[:, :HD]
            stage_f[pl.ds((2 + s) * CELLS + c, NZ, stride=PACK), :] = rows[:, HD:]
    stage[...] = stage_f[...].astype(BF16).reshape(NZ, PACK, HD)

    def packet(e):
        to = lax.rem(me_z + shift_of(e) + NZ, NZ)
        return pltpu.make_async_remote_copy(
            src_ref=stage.at[to], dst_ref=recv.at[mirror(e)], send_sem=a_send.at[e],
            recv_sem=a_recv.at[mirror(e)], device_id={"req": to * 2 + core}, device_id_type=MESH,
        )

    for e in range(NZ - 1, 0, -1):
        packet(e).start()
    recv[0] = stage[me_z]

    row = iota((8, NR * IMG), 0)
    start = jnp.broadcast_to(slot_r[...], (8, NR * IMG))
    half_h = jnp.broadcast_to(grid_r[0:1, :], (8, NR * IMG)) >> 1
    half_w = jnp.broadcast_to(grid_r[1:2, :], (8, NR * IMG)) >> 1
    facts = jnp.where(
        row == 0, start >> 4, jnp.where(row == 1, start & 15, jnp.where(row == 2, half_h, half_w))
    )
    facts = jnp.where(jnp.broadcast_to(req, (8, NR * IMG)) == me_r, facts, 0).astype(F32).astype(BF16)
    seg = ((iota((NR, NR * IMG), 1) >> 5) == iota((NR, NR * IMG), 0)).astype(BF16)
    by_src = dot_nt(facts, seg).astype(BF16)
    src_col = dot_nt(seg, facts)
    start_c = src_col[:, 0:1] * 16.0 + src_col[:, 1:2]
    off = iota((NR, L), 1).astype(F32) - start_c
    free = 1.0 - jnp.max(((off >= 0.0) & (off < float(CELLS))).astype(F32), axis=0, keepdims=True)
    earlier = (iota((L, L), 0) < iota((L, L), 1)).astype(BF16)
    rank = dot(jnp.broadcast_to(free, (8, L)).astype(BF16), earlier)[0:1, :]
    place = iota((L, L), 1)
    rest = (iota((L, L), 0).astype(F32) == jnp.where(free > 0.5, rank, -1.0)).astype(F32)

    n_col = iota((L, 1), 0) - TEXT
    n_row = iota((1, L), 1) - TEXT

    def source(n):
        e, s, c, i, j = cell_of(n)
        mag = (e + 1) >> 1
        z = (me_z + NZ + jnp.where((e & 1) == 1, mag, -mag)) & (NZ - 1)
        return jnp.where(n >= 0, 2 * z + s, -1), c, i, j

    k_col, c_c, i_c, j_c = source(n_col)
    _, c_r, i_r, j_r = source(n_row)
    expand = (k_col == iota((L, NR), 1)).astype(BF16)
    f_col = dot_nt(expand, by_src)
    f_row = dot_nt(by_src, expand)
    pos_c, valid_c = place_of(
        f_col[:, 0:1] * 16.0 + f_col[:, 1:2], f_col[:, 2:3], f_col[:, 3:4], c_c, i_c, j_c
    )
    pos_r, valid_r = place_of(
        f_row[0:1] * 16.0 + f_row[1:2], f_row[2:3], f_row[3:4], c_r, i_r, j_r
    )
    pos_c = jnp.where(n_col >= 0, pos_c, -1.0)
    to_slot[...] = (rest + (place.astype(F32) == pos_c).astype(F32)).astype(BF16)
    p8 = iota((8, L), 1)
    digits = jnp.where(iota((8, L), 0) == 0, p8 >> 4, p8 & 15).astype(F32).astype(BF16)
    rest_r = dot_nt(digits, rest.astype(BF16))
    pos_r = jnp.where(n_row >= 0, pos_r, rest_r[0:1] * 16.0 + rest_r[1:2])
    is_img_r = (n_row >= 0) & valid_r
    bad_r = ((n_row >= 0) & jnp.logical_not(valid_r)).astype(F32)

    gv2 = gv_r[...].astype(F32)
    gv = jnp.concatenate([gv2[0:1], gv2[1:2]], axis=1)
    gd2 = gd_r[...].astype(F32)
    gd_i = iota((D // HD, HD), 0)
    gd = jnp.concatenate(
        [jnp.sum(jnp.where(gd_i == 2 * me_t + h, gd2, 0.0), axis=0, keepdims=True) for h in range(2)],
        axis=1,
    )
    load_t.wait()
    xraw[...] = dot(to_slot[...], text_v[...])

    sel_r, sel_c = iota((GROUP, 4 * PACK), 0), iota((GROUP, 4 * PACK), 1)
    sel_e = (sel_r * 3641) >> 16
    sel_at = sel_e * PACK + sel_r - 18 * sel_e
    left = (sel_c == sel_at).astype(BF16)
    right = (sel_c == sel_at + 18).astype(BF16)

    def two(s, r):
        hi = s.astype(BF16).astype(F32)
        lo = s - hi

        def wide(v):
            return jnp.concatenate([v[:, W:], jnp.zeros((8, 2 * W - L), F32)], axis=1)

        return jnp.where(
            r == 0, hi[:, :W], jnp.where(r == 1, wide(hi), jnp.where(r == 2, lo[:, :W], wide(lo)))
        )

    def fill(b):
        if b == 0:
            x = xraw[:TEXT]
            rows = slice(0, TEXT)
            sq_i[rows] = jnp.zeros((TEXT, W), BF16)
        else:
            for e in range(4 * (b - 1), 4 * b):
                if e:
                    packet(mirror(e)).wait_recv()
            rows = slice(TEXT + GROUP * (b - 1), TEXT + GROUP * b)
            got = recv[4 * (b - 1):4 * b].reshape(4 * PACK, HD)
            img = jnp.concatenate([dot(left, got), dot(right, got)], axis=1)
            x = jnp.where(valid_c[rows], img * gv, xraw[rows])
            xraw[rows] = x
            sq_i[rows] = (img * img).astype(BF16)
        xfull[me_t, rows] = (x * gd).astype(BF16)
        sq_r[rows] = (x * x).astype(BF16)
        if b == len(X_BLOCKS) - 1:
            ones = jnp.ones((8, W), BF16)
            r8 = iota((8, W), 0)
            xfull[me_t, L:] = jnp.where(
                r8 < 4, two(dot_nt(ones, sq_i[...]), r8), two(dot_nt(ones, sq_r[...]), r8 - 4)
            ).astype(BF16)

    def gather(buf, blocks, starts, send, rec, fill, use):
        sent = []

        def copy(da, db, b, ka, kb, k):
            t = at(da, db)
            rows = pl.ds(*blocks[b])
            return pltpu.make_async_remote_copy(
                src_ref=buf.at[t, rows], dst_ref=buf.at[t, rows], send_sem=send.at[k],
                recv_sem=rec.at[t, b], device_id={"tensor": at(ka, kb)}, device_id_type=MESH,
            )

        def push(da, db, b, ka, kb):
            one = copy(da, db, b, ka, kb, len(sent))
            one.start()
            sent.append(one)

        def wait(da, db, b):
            copy(da, db, b, 0, 1, 0).wait_recv()

        def turn(column, b):
            return 1 - 2 * lax.rem(pb + column + b, 2)

        def both(da, b):
            push(da, 0, b, 0, 1)
            push(da, 0, b, 0, -1)

        def around(da, b):
            wait(da, -1, b)
            wait(da, 1, b)
            s = turn(pa + da + 4, b)
            push(da, -s, b, 0, s)

        for b, p in order(starts):
            if p == 0:
                fill(b)
                push(0, 0, b, 1, 0)
                push(0, 0, b, -1, 0)
                both(0, b)
                new = ((0, 0),)
            elif p == 1:
                wait(-1, 0, b)
                wait(1, 0, b)
                s = turn(pa, b)
                push(-s, 0, b, s, 0)
                both(-1, b)
                both(1, b)
                around(0, b)
                new = ((-1, 0), (1, 0), (0, -1), (0, 1))
            elif p == 2:
                wait(2, 0, b)
                both(2, b)
                around(-1, b)
                around(1, b)
                wait(0, 2, b)
                new = ((2, 0), (-1, -1), (-1, 1), (1, -1), (1, 1), (0, 2))
            elif p == 3:
                around(2, b)
                wait(-1, 2, b)
                wait(1, 2, b)
                new = ((2, -1), (2, 1), (-1, 2), (1, 2))
            else:
                wait(2, 2, b)
                new = ((2, 2),)
            use(b, p, [at(*one) for one in new])
        return sent

    def w_copy(d):
        to = lax.rem(me_t + d, NT)
        return pltpu.make_async_remote_copy(
            src_ref=wout_h.at[half, w_cols(to)], dst_ref=wcol.at[me_t, half],
            send_sem=w_send.at[d], recv_sem=w_recv.at[me_t], device_id={"tensor": to},
            device_id_type=MESH,
        )

    def w_wait(d):
        frm = lax.rem(me_t + d, NT)
        pltpu.make_async_remote_copy(
            src_ref=wcol.at[frm, half], dst_ref=wcol.at[frm, half], send_sem=w_send.at[d],
            recv_sem=w_recv.at[frm], device_id={"tensor": frm}, device_id_type=MESH,
        ).wait_recv()

    w_swap = pltpu.make_async_remote_copy(
        src_ref=wcol.at[:, half], dst_ref=wcol.at[:, half], send_sem=p_sem.at[2],
        recv_sem=p_sem.at[3], device_id={"req": sibling}, device_id_type=MESH,
    )
    last = len(X_BLOCKS) - 1
    early = X_BLOCKS[last][0]

    def project(b, p, chunks):
        if b == 0 and p == 0:
            for d in range(1, NT):
                w_copy(d).start()
            for one in load_w:
                one.wait()
            acc[...] = jnp.zeros_like(acc)
            stat[...] = jnp.zeros_like(stat)
            row = iota((L, L), 0).astype(F32)
            to_pos[...] = (row == pos_r).astype(BF16)
        if b == last and p == 0:
            load_o.wait()
            for d in range(1, NT):
                w_wait(d)
            w_swap.start()
        for t in chunks:
            w_rows = pl.ds(pl.multiple_of(t * W, W), W)
            if b == last - 1:
                acc[:early] += dot(xfull[t, :early], w_v[w_rows, :])
            if b == last:
                acc[early:] += dot(xfull[t, early:L], w_v[w_rows, :])
                stat[...] += xfull[t, L:].astype(F32)

    x_sent = gather(xfull, X_BLOCKS, X_START, x_send, x_recv, fill, project)

    sums = stat[...]

    def whole(r):
        return jnp.concatenate(
            [sums[r:r + 1, :] + sums[r + 2:r + 3, :],
             sums[r + 1:r + 2, :L - W] + sums[r + 3:r + 4, :L - W]], axis=1
        )

    rv = jnp.where(is_img_r, lax.rsqrt(whole(0) / D + EPS), 1.0)
    rd = lax.rsqrt(rv * rv * whole(4) / D + EPS)
    cols = jnp.transpose(jnp.where(iota((8, L), 0) == 0, rv * rd, rv))
    qkv = (acc[...] * cols[:, 0:1]).astype(BF16)
    queries = dot(to_pos[...], qkv[:, :HD]).astype(BF16)

    def attend(b):
        rows = slice(C_BLOCKS[b][0], C_BLOCKS[b][0] + C_BLOCKS[b][1])
        scores = dot_nt(queries[rows], qkv[:, HD:2 * HD]) * (HD ** -0.5)
        at_q = (iota((C_BLOCKS[b][1], L), 0) + C_BLOCKS[b][0]).astype(F32)
        scores = jnp.where((at_q >= pos_r) & (bad_r < 0.5), scores, -1e30)
        expo = jnp.exp(scores - jnp.max(scores, axis=-1, keepdims=True))
        probs = (expo / jnp.sum(expo, axis=-1, keepdims=True)).astype(BF16)
        cfull[me_t, rows] = dot(probs, qkv[:, 2 * HD:]).astype(BF16)

    def combine(b, p, chunks):
        if b == 1 and p == 0:
            x_in = (xraw[...] * cols[:, 1:2]).astype(BF16)
            oacc[...] = dot(to_pos[...], x_in)
            w_swap.wait_recv()
        if b == 1:
            for t in chunks:
                oacc[...] += dot(cfull[t], wcol[t])

    c_sent = gather(cfull, C_BLOCKS, C_START, c_send, c_recv, attend, combine)
    out_r[...] = oacc[...].astype(BF16)

    swap.wait_send()
    w_swap.wait_send()
    for e in range(1, NZ):
        packet(e).wait_send()
    for d in range(1, NT):
        w_copy(d).wait_send()
    for one in x_sent + c_sent:
        one.wait_send()


def body(text, patches, grids, image_request, slot_start, vis_gain, dec_gain, w_qkv, w_out):
    vmem = pl.BlockSpec(memory_space=pltpu.VMEM)
    hbm = pl.BlockSpec(memory_space=pl.ANY)
    dma = pltpu.SemaphoreType.DMA
    return pl.pallas_call(
        kernel,
        out_shape=jax.ShapeDtypeStruct((L, W), BF16),
        in_specs=[hbm, hbm, vmem, vmem, vmem, vmem, vmem, hbm, hbm],
        out_specs=vmem,
        scratch_shapes=[
            pltpu.VMEM((L, W), BF16),
            pltpu.VMEM((6, 6, IMG, W), BF16),
            pltpu.VMEM((D, 3 * HD), BF16),
            pltpu.VMEM((NT, HD, W), BF16),
            pltpu.VMEM((CELLS, 2, IMG, W), BF16),
            pltpu.VMEM((NZ * PACK, HD), F32),
            pltpu.VMEM((NZ, PACK, HD), BF16),
            pltpu.VMEM((NZ, PACK, HD), BF16),
            pltpu.VMEM((L, L), BF16),
            pltpu.VMEM((L, L), BF16),
            pltpu.VMEM((L, W), F32),
            pltpu.VMEM((L, W), BF16),
            pltpu.VMEM((L, W), BF16),
            pltpu.VMEM((NT, L + 8, W), BF16),
            pltpu.VMEM((NT, L, HD), BF16),
            pltpu.VMEM((L, 3 * HD), F32),
            pltpu.VMEM((L, W), F32),
            pltpu.VMEM((8, W), F32),
            dma((6,)), dma((4,)), dma((NT,)), dma((NT,)), dma((NZ,)), dma((NZ,)),
            dma((15 * len(X_BLOCKS),)), dma((NT, len(X_BLOCKS))),
            dma((15 * len(C_BLOCKS),)), dma((NT, len(C_BLOCKS))),
        ],
        compiler_params=pltpu.CompilerParams(
            collective_id=0, has_side_effects=True, vmem_limit_bytes=62 * 2**20
        ),
    )(
        text,
        patches.transpose(1, 2, 0, 3),
        grids.T,
        image_request.reshape(1, -1),
        slot_start.reshape(1, -1),
        vis_gain.reshape(-1, HD),
        dec_gain.reshape(-1, HD),
        w_qkv.transpose(1, 0, 2),
        w_out,
    )


def solution(mesh):
    in_specs = (
        P("req", "tensor"),
        P("req", None, None, "tensor"),
        P(),
        P(),
        P(),
        P("tensor"),
        P(),
        P(None, None, "tensor"),
        P("tensor", None),
    )
    return jax.shard_map(
        body, mesh=mesh, in_specs=in_specs, out_specs=P("req", "tensor"), check_vma=False
    )
```

```python
import jax
import jax.numpy as jnp
from jax import lax
from jax.experimental import pallas as pl
from jax.experimental.pallas import tpu as pltpu
from jax.sharding import PartitionSpec as P

D = 4096
HD = 128
L = 384
W = 256
NR = 32
NZ = 16
NT = 16
IMG = 32
CELLS = 9
TEXT = L - NR * CELLS
PACK = 40
GROUP = 72
EPS = 1e-05
MESH = pl.DeviceIdType.MESH
F32 = jnp.float32
BF16 = jnp.bfloat16
EARLY, SPLIT = TEXT, TEXT + 2 * GROUP
X_PARTS = ((0, EARLY), (EARLY, SPLIT - EARLY), (SPLIT, L + 8 - SPLIT))
Q_PARTS = ((0, L // 2), (L // 2, L // 2))
PEERS = (2, 1, -1)


def iota(shape, dim):
    return lax.broadcasted_iota(jnp.int32, shape, dim)


def dot(a, b):
    return lax.dot_general(a, b, (((1,), (0,)), ((), ())), preferred_element_type=F32)


def dot_nt(a, b):
    return lax.dot_general(a, b, (((1,), (1,)), ((), ())), preferred_element_type=F32)


def shift_of(e):
    return (e + 1) // 2 if e % 2 else -(e // 2)


def mirror(e):
    return e if e in (0, NZ - 1) else (e + 1 if e % 2 else e - 1)


def cell_of(n):
    e = (n * 3641) >> 16
    q = n - 18 * e
    s = (q >= CELLS).astype(jnp.int32)
    c = q - CELLS * s
    i = (c >= 3).astype(jnp.int32) + (c >= 6).astype(jnp.int32)
    return e, s, c.astype(F32), i.astype(F32), (c - 3 * i).astype(F32)


def place_of(start, hh, hw, c, i, j):
    valid = (i < hh) & (j < hw)
    before = jnp.minimum(i, hh) * hw + jnp.where(i < hh, jnp.minimum(j, hw), 0.0)
    return start + jnp.where(valid, i * hw + j, hh * hw + c - before), valid


def kernel(
    text_h, patch_h, grid_r, req_r, slot_r, gv_r, gd_r, wqkv_h, wout_h, out_r,
    text_v, patch_v, w_v, w_blk, pool, stage_f, stage, recv, to_slot, to_pos, xraw, sq_i, sq_r,
    xfull, ctx, part, part_in, acc, oacc, stat, loc_sem, p_sem, w_send, w_recv, a_send, a_recv,
    x_send, x_recv, c_send, c_recv, o_send, o_recv,
):
    me_r = lax.axis_index("req")
    me_t = lax.axis_index("tensor")
    core = me_r & 1
    me_z = me_r >> 1
    sibling = me_r + 1 - 2 * core
    tx, ty = me_t & 3, me_t >> 2
    pa, pb = tx + core * (ty - tx), ty + core * (tx - ty)
    sa, sb = 1 + 3 * core, 4 - 3 * core
    ids = {
        (da, db): ((pa + da) & 3) * sa + ((pb + db) & 3) * sb for da in range(4) for db in range(4)
    }

    def at(da, db):
        return ids[da % 4, db % 4]

    def z_peer(shift):
        return ((me_z + shift + NZ) & (NZ - 1)) * 2 + core

    def w_cols(t):
        return pl.ds(pl.multiple_of(t * W, W), W)

    heads = pl.ds(pl.multiple_of(pa * HD, HD), HD)

    load_p = pltpu.make_async_copy(patch_h, patch_v, loc_sem.at[0])
    load_t = pltpu.make_async_copy(text_h, text_v, loc_sem.at[1])
    load_w = [
        pltpu.make_async_copy(wqkv_h.at[j], w_v.at[:, pl.ds(j * HD, HD)], loc_sem.at[2 + j])
        for j in range(3)
    ]
    load_o = [
        pltpu.make_async_copy(
            wout_h.at[:, w_cols(at(0, db))], w_blk.at[(pb + db) & 3, heads], loc_sem.at[5 + db]
        )
        for db in range(4)
    ]
    load_p.start()
    barrier = pltpu.get_barrier_semaphore()

    def greet(**device):
        pl.semaphore_signal(barrier, inc=1, device_id=device, device_id_type=MESH)

    for e in range(NZ - 1, 0, -1):
        greet(req=z_peer(shift_of(e)))
    greet(req=sibling)
    for d in PEERS:
        greet(tensor=at(d, 0))
        greet(tensor=at(0, d))
    load_t.start()
    for copy in load_o + load_w:
        copy.start()

    req = req_r[...]
    req8 = jnp.broadcast_to(req.astype(F32), (8, NR * IMG)).astype(BF16)
    ours = (
        iota((2 * IMG, NR * IMG), 1) == me_z * 2 * IMG + iota((2 * IMG, NR * IMG), 0)
    ).astype(BF16)
    goes = dot_nt(req8, ours)[0:1, :]
    row_s = (iota((NR, 2 * IMG), 0) >= NZ).astype(jnp.int32)
    col_s = (iota((NR, 2 * IMG), 1) >= IMG).astype(jnp.int32)
    wanted = ((iota((NR, 2 * IMG), 0) - NZ * row_s) * 2 + core).astype(F32)
    pick = ((row_s == col_s) & (wanted == goes)).astype(BF16)

    load_p.wait()
    for c in range(CELLS):
        i, j = 2 * (c // 3), 2 * (c % 3)
        total = (
            patch_v[i, j].astype(F32) + patch_v[i, j + 1].astype(F32)
            + patch_v[i + 1, j].astype(F32) + patch_v[i + 1, j + 1].astype(F32)
        )
        pool[c, core] = (total * 0.25).astype(BF16)
    stage_f[...] = jnp.zeros_like(stage_f)

    pl.semaphore_wait(barrier, NZ - 1 + 1 + 2 * len(PEERS))

    swap = pltpu.make_async_remote_copy(
        src_ref=pool.at[:, core], dst_ref=pool.at[:, core], send_sem=p_sem.at[0],
        recv_sem=p_sem.at[1], device_id={"req": sibling}, device_id_type=MESH,
    )
    swap.start()
    swap.wait_recv()
    for c in range(CELLS):
        sent = dot(pick, pool[c].reshape(2 * IMG, W))
        for s in range(2):
            rows = sent[s * NZ:(s + 1) * NZ]
            stage_f[pl.ds(s * CELLS + c, NZ, stride=PACK), :] = rows[:, :HD]
            stage_f[pl.ds((2 + s) * CELLS + c, NZ, stride=PACK), :] = rows[:, HD:]
    stage[...] = stage_f[...].astype(BF16).reshape(NZ, PACK, HD)

    def packet(e):
        to = (me_z + shift_of(e) + NZ) & (NZ - 1)
        return pltpu.make_async_remote_copy(
            src_ref=stage.at[to], dst_ref=recv.at[mirror(e)], send_sem=a_send.at[e],
            recv_sem=a_recv.at[mirror(e)], device_id={"req": to * 2 + core}, device_id_type=MESH,
        )

    for e in range(NZ - 1, 0, -1):
        packet(e).start()
    recv[0] = stage[me_z]

    row = iota((8, NR * IMG), 0)
    start = jnp.broadcast_to(slot_r[...], (8, NR * IMG))
    half_h = jnp.broadcast_to(grid_r[0:1, :], (8, NR * IMG)) >> 1
    half_w = jnp.broadcast_to(grid_r[1:2, :], (8, NR * IMG)) >> 1
    facts = jnp.where(
        row == 0, start >> 4, jnp.where(row == 1, start & 15, jnp.where(row == 2, half_h, half_w))
    )
    facts = jnp.where(jnp.broadcast_to(req, (8, NR * IMG)) == me_r, facts, 0).astype(F32).astype(BF16)
    seg = ((iota((NR, NR * IMG), 1) >> 5) == iota((NR, NR * IMG), 0)).astype(BF16)
    by_src = dot_nt(facts, seg).astype(BF16)
    src_col = dot_nt(seg, facts)
    start_c = src_col[:, 0:1] * 16.0 + src_col[:, 1:2]
    off = iota((NR, L), 1).astype(F32) - start_c
    free = 1.0 - jnp.max(((off >= 0.0) & (off < float(CELLS))).astype(F32), axis=0, keepdims=True)
    earlier = (iota((L, L), 0) < iota((L, L), 1)).astype(BF16)
    rank = dot(jnp.broadcast_to(free, (8, L)).astype(BF16), earlier)[0:1, :]
    place = iota((L, L), 1)
    rest = (iota((L, L), 0).astype(F32) == jnp.where(free > 0.5, rank, -1.0)).astype(F32)

    n_col = iota((L, 1), 0) - TEXT
    n_row = iota((1, L), 1) - TEXT

    def source(n):
        e, s, c, i, j = cell_of(n)
        mag = (e + 1) >> 1
        z = (me_z + NZ + jnp.where((e & 1) == 1, mag, -mag)) & (NZ - 1)
        return jnp.where(n >= 0, 2 * z + s, -1), c, i, j

    k_col, c_c, i_c, j_c = source(n_col)
    _, c_r, i_r, j_r = source(n_row)
    expand = (k_col == iota((L, NR), 1)).astype(BF16)
    f_col = dot_nt(expand, by_src)
    f_row = dot_nt(by_src, expand)
    pos_c, valid_c = place_of(
        f_col[:, 0:1] * 16.0 + f_col[:, 1:2], f_col[:, 2:3], f_col[:, 3:4], c_c, i_c, j_c
    )
    pos_r, valid_r = place_of(
        f_row[0:1] * 16.0 + f_row[1:2], f_row[2:3], f_row[3:4], c_r, i_r, j_r
    )
    pos_c = jnp.where(n_col >= 0, pos_c, -1.0)
    to_slot[...] = (rest + (place.astype(F32) == pos_c).astype(F32)).astype(BF16)
    p8 = iota((8, L), 1)
    digits = jnp.where(iota((8, L), 0) == 0, p8 >> 4, p8 & 15).astype(F32).astype(BF16)
    rest_r = dot_nt(digits, rest.astype(BF16))
    pos_r = jnp.where(n_row >= 0, pos_r, rest_r[0:1] * 16.0 + rest_r[1:2])
    is_img_r = (n_row >= 0) & valid_r
    bad_r = ((n_row >= 0) & jnp.logical_not(valid_r)).astype(F32)

    gv2 = gv_r[...].astype(F32)
    gv = jnp.concatenate([gv2[0:1], gv2[1:2]], axis=1)
    gd2 = gd_r[...].astype(F32)
    gd_i = iota((D // HD, HD), 0)
    gd = jnp.concatenate(
        [jnp.sum(jnp.where(gd_i == 2 * me_t + h, gd2, 0.0), axis=0, keepdims=True) for h in range(2)],
        axis=1,
    )
    load_t.wait()
    xraw[...] = dot(to_slot[...], text_v[...])

    sel_r, sel_c = iota((GROUP, 4 * PACK), 0), iota((GROUP, 4 * PACK), 1)
    sel_e = (sel_r * 3641) >> 16
    sel_at = sel_e * PACK + sel_r - 18 * sel_e
    left = (sel_c == sel_at).astype(BF16)
    right = (sel_c == sel_at + 18).astype(BF16)

    def two(s, r):
        hi = s.astype(BF16).astype(F32)
        lo = s - hi

        def wide(v):
            return jnp.concatenate([v[:, W:], jnp.zeros((8, 2 * W - L), F32)], axis=1)

        return jnp.where(
            r == 0, hi[:, :W], jnp.where(r == 1, wide(hi), jnp.where(r == 2, lo[:, :W], wide(lo)))
        )

    def put(x, rows):
        xfull[me_t, rows] = (x * gd).astype(BF16)
        sq_r[rows] = (x * x).astype(BF16)

    def fill(g):
        for e in range(4 * g, 4 * g + 4):
            if e:
                packet(mirror(e)).wait_recv()
        rows = slice(TEXT + GROUP * g, TEXT + GROUP * (g + 1))
        got = recv[4 * g:4 * g + 4].reshape(4 * PACK, HD)
        img = jnp.concatenate([dot(left, got), dot(right, got)], axis=1)
        x = jnp.where(valid_c[rows], img * gv, xraw[rows])
        xraw[rows] = x
        sq_i[rows] = (img * img).astype(BF16)
        put(x, rows)

    sent = []

    def x_copy(da, db, h, ka, kb, k):
        t = at(da, db)
        rows = pl.ds(*X_PARTS[h])
        return pltpu.make_async_remote_copy(
            src_ref=xfull.at[t, rows], dst_ref=xfull.at[t, rows], send_sem=x_send.at[k],
            recv_sem=x_recv.at[t, h], device_id={"tensor": at(ka, kb)}, device_id_type=MESH,
        )

    def push(da, db, h, *to):
        for ka, kb in to:
            one = x_copy(da, db, h, ka, kb, len(sent))
            one.start()
            sent.append(one)

    def wait(da, db, h):
        x_copy(da, db, h, 0, 1, 0).wait_recv()

    def w_copy(i, db):
        return pltpu.make_async_remote_copy(
            src_ref=wout_h.at[:, w_cols(at(PEERS[i], db))], dst_ref=w_blk.at[(pb + db) & 3, heads],
            send_sem=w_send.at[i, db], recv_sem=w_recv.at[i, db],
            device_id={"tensor": at(PEERS[i], 0)}, device_id_type=MESH,
        )

    def w_wait(i, db):
        rows = pl.ds(pl.multiple_of(((pa - PEERS[i]) & 3) * HD, HD), HD)
        block = w_blk.at[(pb + db) & 3, rows]
        pltpu.make_async_remote_copy(
            src_ref=block, dst_ref=block, send_sem=w_send.at[i, db], recv_sem=w_recv.at[i, db],
            device_id={"tensor": at(-PEERS[i], 0)}, device_id_type=MESH,
        ).wait_recv()

    sq_i[:TEXT] = jnp.zeros((TEXT, W), BF16)
    put(xraw[:TEXT], slice(0, TEXT))
    ring_b = tuple((0, d) for d in PEERS)
    push(0, 0, 0, *((d, 0) for d in PEERS), *ring_b)
    for i in range(len(PEERS)):
        for db in range(4):
            w_copy(i, db).start()
    to_pos[...] = (iota((L, L), 0).astype(F32) == pos_r).astype(BF16)
    stat[...] = jnp.zeros_like(stat)
    acc[...] = jnp.zeros_like(acc)
    for da in PEERS[::-1]:
        wait(da, 0, 0)
        push(da, 0, 0, *ring_b)

    up_a, dn_a, up_b, dn_b = (1, 0), (-1, 0), (0, 1), (0, -1)
    fill(0)
    fill(1)
    push(0, 0, 1, up_a, dn_a, up_b, dn_b)
    fill(2)
    fill(3)
    ones = jnp.ones((8, W), BF16)
    r8 = iota((8, W), 0)
    xfull[me_t, L:] = jnp.where(
        r8 < 4, two(dot_nt(ones, sq_i[...]), r8), two(dot_nt(ones, sq_r[...]), r8 - 4)
    ).astype(BF16)
    push(0, 0, 2, up_a, dn_a, up_b, dn_b)

    def project(da, db):
        if db:
            wait(da, db, 0)
        t = at(da, db)
        acc[...] += dot(xfull[t, :L], w_v[pl.ds(pl.multiple_of(t * W, W), W), :])
        stat[...] += xfull[t, L:].astype(F32)

    for one in load_w:
        one.wait()
    project(0, 0)
    wait(-1, 0, 1)
    push(-1, 0, 1, up_a, up_b, dn_b)
    wait(1, 0, 1)
    push(1, 0, 1, up_b, dn_b)
    wait(0, -1, 1)
    push(0, -1, 1, up_b)
    wait(0, 1, 1)
    wait(1, 0, 2)
    push(1, 0, 2, dn_a, up_b, dn_b)
    wait(-1, 0, 2)
    push(-1, 0, 2, up_b, dn_b)
    wait(0, 1, 2)
    push(0, 1, 2, dn_b)
    wait(0, -1, 2)
    project(1, 0)
    project(-1, 0)
    for h in (1, 2):
        wait(2, 0, h)
        push(2, 0, h, up_b, dn_b)
    for da in (-1, 1):
        wait(da, -1, 1)
        push(da, -1, 1, up_b)
        wait(da, 1, 1)
    for da in (-1, 1):
        wait(da, 1, 2)
        push(da, 1, 2, dn_b)
        wait(da, -1, 2)
    wait(0, 2, 1)
    wait(0, 2, 2)
    for one in ((0, 1), (0, -1), (2, 0), (0, 2), (1, 1), (1, -1)):
        project(*one)
    wait(2, -1, 1)
    push(2, -1, 1, up_b)
    wait(2, 1, 1)
    wait(2, 1, 2)
    push(2, 1, 2, dn_b)
    wait(2, -1, 2)
    project(-1, 1)
    project(-1, -1)
    project(2, 1)
    project(2, -1)
    for da in (-1, 1):
        wait(da, 2, 1)
        wait(da, 2, 2)
        project(da, 2)
    for one in load_o:
        one.wait()
    for i in range(len(PEERS)):
        for db in range(4):
            w_wait(i, db)
    wait(2, 2, 1)
    wait(2, 2, 2)
    project(2, 2)

    sums = stat[...]

    def whole(r):
        return jnp.concatenate(
            [sums[r:r + 1, :] + sums[r + 2:r + 3, :],
             sums[r + 1:r + 2, :L - W] + sums[r + 3:r + 4, :L - W]], axis=1
        )

    rv = jnp.where(is_img_r, lax.rsqrt(whole(0) / D + EPS), 1.0)
    rd = lax.rsqrt(rv * rv * whole(4) / D + EPS)
    cols = jnp.transpose(jnp.where(iota((8, L), 0) == 0, rv * rd, rv))
    qkv = (acc[...] * cols[:, 0:1]).astype(BF16)
    queries = dot(to_pos[...], qkv[:, :HD]).astype(BF16)

    def c_copy(b, i):
        block = ctx.at[pl.ds(*Q_PARTS[b]), heads]
        return pltpu.make_async_remote_copy(
            src_ref=block, dst_ref=block, send_sem=c_send.at[b, i], recv_sem=c_recv.at[b, i],
            device_id={"tensor": at(PEERS[i], 0)}, device_id_type=MESH,
        )

    def c_wait(b, i):
        cols = pl.ds(pl.multiple_of(((pa - PEERS[i]) & 3) * HD, HD), HD)
        block = ctx.at[pl.ds(*Q_PARTS[b]), cols]
        pltpu.make_async_remote_copy(
            src_ref=block, dst_ref=block, send_sem=c_send.at[b, i], recv_sem=c_recv.at[b, i],
            device_id={"tensor": at(-PEERS[i], 0)}, device_id_type=MESH,
        ).wait_recv()

    def o_copy(b, i):
        rows = pl.ds(*Q_PARTS[b])
        return pltpu.make_async_remote_copy(
            src_ref=part.at[i, rows], dst_ref=part_in.at[i, rows], send_sem=o_send.at[b, i],
            recv_sem=o_recv.at[b, i], device_id={"tensor": at(0, PEERS[i])}, device_id_type=MESH,
        )

    both = [(b, i) for b in range(len(Q_PARTS)) for i in range(len(PEERS))]
    for b, (lo, n) in enumerate(Q_PARTS):
        scores = dot_nt(queries[lo:lo + n], qkv[:, HD:2 * HD]) * (HD ** -0.5)
        at_q = (iota((n, L), 0) + lo).astype(F32)
        scores = jnp.where((at_q >= pos_r) & (bad_r < 0.5), scores, -1e30)
        expo = jnp.exp(scores - jnp.max(scores, axis=-1, keepdims=True))
        probs = (expo / jnp.sum(expo, axis=-1, keepdims=True)).astype(BF16)
        ctx[lo:lo + n, heads] = dot(probs, qkv[:, 2 * HD:]).astype(BF16)
        for i in range(len(PEERS)):
            c_copy(b, i).start()
    oacc[...] = dot(to_pos[...], (xraw[...] * cols[:, 1:2]).astype(BF16))
    for b, (lo, n) in enumerate(Q_PARTS):
        for i in range(len(PEERS)):
            c_wait(b, i)
        for i, db in enumerate(PEERS):
            part[i, lo:lo + n] = dot(ctx[lo:lo + n], w_blk[(pb + db) & 3]).astype(BF16)
            o_copy(b, i).start()
    for b, (lo, n) in enumerate(Q_PARTS):
        oacc[lo:lo + n] += dot(ctx[lo:lo + n], w_blk[pb])
    for b, (lo, n) in enumerate(Q_PARTS):
        total = oacc[lo:lo + n]
        for i in range(len(PEERS)):
            o_copy(b, i).wait_recv()
            total = total + part_in[i, lo:lo + n].astype(F32)
        out_r[lo:lo + n] = total.astype(BF16)

    swap.wait_send()
    for e in range(1, NZ):
        packet(e).wait_send()
    for i in range(len(PEERS)):
        for db in range(4):
            w_copy(i, db).wait_send()
    for b, i in both:
        c_copy(b, i).wait_send()
        o_copy(b, i).wait_send()
    for one in sent:
        one.wait_send()


def body(text, patches, grids, image_request, slot_start, vis_gain, dec_gain, w_qkv, w_out):
    vmem = pl.BlockSpec(memory_space=pltpu.VMEM)
    hbm = pl.BlockSpec(memory_space=pl.ANY)
    dma = pltpu.SemaphoreType.DMA
    return pl.pallas_call(
        kernel,
        out_shape=jax.ShapeDtypeStruct((L, W), BF16),
        in_specs=[hbm, hbm, vmem, vmem, vmem, vmem, vmem, hbm, hbm],
        out_specs=vmem,
        scratch_shapes=[
            pltpu.VMEM((L, W), BF16),
            pltpu.VMEM((6, 6, IMG, W), BF16),
            pltpu.VMEM((D, 3 * HD), BF16),
            pltpu.VMEM((4, 4 * HD, W), BF16),
            pltpu.VMEM((CELLS, 2, IMG, W), BF16),
            pltpu.VMEM((NZ * PACK, HD), F32),
            pltpu.VMEM((NZ, PACK, HD), BF16),
            pltpu.VMEM((NZ, PACK, HD), BF16),
            pltpu.VMEM((L, L), BF16),
            pltpu.VMEM((L, L), BF16),
            pltpu.VMEM((L, W), F32),
            pltpu.VMEM((L, W), BF16),
            pltpu.VMEM((L, W), BF16),
            pltpu.VMEM((NT, L + 8, W), BF16),
            pltpu.VMEM((L, 4 * HD), BF16),
            pltpu.VMEM((3, L, W), BF16),
            pltpu.VMEM((3, L, W), BF16),
            pltpu.VMEM((L, 3 * HD), F32),
            pltpu.VMEM((L, W), F32),
            pltpu.VMEM((8, W), F32),
            dma((9,)), dma((2,)), dma((3, 4)), dma((3, 4)), dma((NZ,)), dma((NZ,)),
            dma((48,)), dma((NT, 3)), dma((2, 3)), dma((2, 3)), dma((2, 3)), dma((2, 3)),
        ],
        compiler_params=pltpu.CompilerParams(
            collective_id=0, has_side_effects=True, vmem_limit_bytes=62 * 2**20
        ),
    )(
        text,
        patches.transpose(1, 2, 0, 3),
        grids.T,
        image_request.reshape(1, -1),
        slot_start.reshape(1, -1),
        vis_gain.reshape(-1, HD),
        dec_gain.reshape(-1, HD),
        w_qkv.transpose(1, 0, 2),
        w_out,
    )


def solution(mesh):
    in_specs = (
        P("req", "tensor"),
        P("req", None, None, "tensor"),
        P(),
        P(),
        P(),
        P("tensor"),
        P(),
        P(None, None, "tensor"),
        P("tensor", None),
    )
    return jax.shard_map(
        body, mesh=mesh, in_specs=in_specs, out_specs=P("req", "tensor"), check_vma=False
    )
```

```python
import jax
import jax.numpy as jnp
from jax import lax
from jax.experimental import pallas as pl
from jax.experimental.pallas import tpu as pltpu
from jax.sharding import PartitionSpec as P

D = 4096
HD = 128
L = 384
W = 256
NR = 32
NZ = 16
NT = 16
IMG = 32
CELLS = 9
TEXT = L - NR * CELLS
PACK = 40
GROUP = 72
EPS = 1e-05
MESH = pl.DeviceIdType.MESH
F32 = jnp.float32
BF16 = jnp.bfloat16
EARLY, SPLIT = TEXT, TEXT + 2 * GROUP
X_PARTS = ((0, EARLY), (EARLY, SPLIT - EARLY), (SPLIT, L + 8 - SPLIT))
Q_PARTS = ((0, L // 2), (L // 2, L // 2))
PEERS = (2, 1, -1)


def iota(shape, dim):
    return lax.broadcasted_iota(jnp.int32, shape, dim)


def dot(a, b):
    return lax.dot_general(a, b, (((1,), (0,)), ((), ())), preferred_element_type=F32)


def dot_nt(a, b):
    return lax.dot_general(a, b, (((1,), (1,)), ((), ())), preferred_element_type=F32)


def shift_of(e):
    return (e + 1) // 2 if e % 2 else -(e // 2)


def mirror(e):
    return e if e in (0, NZ - 1) else (e + 1 if e % 2 else e - 1)


def cell_of(n):
    e = (n * 3641) >> 16
    q = n - 18 * e
    s = (q >= CELLS).astype(jnp.int32)
    c = q - CELLS * s
    i = (c >= 3).astype(jnp.int32) + (c >= 6).astype(jnp.int32)
    return e, s, c.astype(F32), i.astype(F32), (c - 3 * i).astype(F32)


def place_of(start, hh, hw, c, i, j):
    valid = (i < hh) & (j < hw)
    before = jnp.minimum(i, hh) * hw + jnp.where(i < hh, jnp.minimum(j, hw), 0.0)
    return start + jnp.where(valid, i * hw + j, hh * hw + c - before), valid


def kernel(
    text_h, patch_h, grid_r, req_r, slot_r, gv_r, gd_r, wqkv_h, wout_h, out_r,
    text_v, patch_v, w_v, w_blk, pool, stage_f, stage, recv, to_slot, to_pos, xraw, sq_i, sq_r,
    xfull, ctx, part, part_in, acc, oacc, stat, loc_sem, p_sem, w_send, w_recv, a_send, a_recv,
    x_send, x_recv, c_send, c_recv, o_send, o_recv,
):
    me_r = lax.axis_index("req")
    me_t = lax.axis_index("tensor")
    core = me_r & 1
    me_z = me_r >> 1
    sibling = me_r + 1 - 2 * core
    tx, ty = me_t & 3, me_t >> 2
    pa, pb = tx + core * (ty - tx), ty + core * (tx - ty)
    sa, sb = 1 + 3 * core, 4 - 3 * core
    ids = {
        (da, db): ((pa + da) & 3) * sa + ((pb + db) & 3) * sb for da in range(4) for db in range(4)
    }

    def at(da, db):
        return ids[da % 4, db % 4]

    def z_peer(shift):
        return ((me_z + shift + NZ) & (NZ - 1)) * 2 + core

    def w_cols(t):
        return pl.ds(pl.multiple_of(t * W, W), W)

    heads = pl.ds(pl.multiple_of(pa * HD, HD), HD)

    load_p = pltpu.make_async_copy(patch_h, patch_v, loc_sem.at[0])
    load_t = pltpu.make_async_copy(text_h, text_v, loc_sem.at[1])
    load_w = [
        pltpu.make_async_copy(wqkv_h.at[j], w_v.at[:, pl.ds(j * HD, HD)], loc_sem.at[2 + j])
        for j in range(3)
    ]
    load_o = [
        pltpu.make_async_copy(
            wout_h.at[:, w_cols(at(0, db))], w_blk.at[(pb + db) & 3, heads], loc_sem.at[5 + db]
        )
        for db in range(4)
    ]
    load_p.start()
    barrier = pltpu.get_barrier_semaphore()

    def greet(**device):
        pl.semaphore_signal(barrier, inc=1, device_id=device, device_id_type=MESH)

    for e in range(NZ - 1, 0, -1):
        greet(req=z_peer(shift_of(e)))
    greet(req=sibling)
    for d in PEERS:
        greet(tensor=at(d, 0))
        greet(tensor=at(0, d))
    load_t.start()
    for copy in load_o + load_w:
        copy.start()

    req = req_r[...]
    req8 = jnp.broadcast_to(req.astype(F32), (8, NR * IMG)).astype(BF16)

    def pack(s):
        first = (me_z * 2 + s) * IMG
        ours = (iota((IMG, NR * IMG), 1) == first + iota((IMG, NR * IMG), 0)).astype(BF16)
        goes = dot_nt(req8, ours)[0:1, :]
        return ((iota((NZ, IMG), 0) * 2 + core).astype(F32) == goes).astype(BF16)

    def stage_rows(s, pick):
        for c in range(CELLS):
            rows = dot(pick, pool[c, s])
            stage_f[pl.ds(s * CELLS + c, NZ, stride=PACK), :] = rows[:, :HD]
            stage_f[pl.ds((2 + s) * CELLS + c, NZ, stride=PACK), :] = rows[:, HD:]

    load_p.wait()
    for c in range(CELLS):
        i, j = 2 * (c // 3), 2 * (c % 3)
        total = (
            patch_v[i, j].astype(F32) + patch_v[i, j + 1].astype(F32)
            + patch_v[i + 1, j].astype(F32) + patch_v[i + 1, j + 1].astype(F32)
        )
        pool[c, core] = (total * 0.25).astype(BF16)
    stage_f[...] = jnp.zeros_like(stage_f)

    stage_rows(core, pack(core))
    other = pack(1 - core)

    row = iota((8, NR * IMG), 0)
    start = jnp.broadcast_to(slot_r[...], (8, NR * IMG))
    half_h = jnp.broadcast_to(grid_r[0:1, :], (8, NR * IMG)) >> 1
    half_w = jnp.broadcast_to(grid_r[1:2, :], (8, NR * IMG)) >> 1
    facts = jnp.where(
        row == 0, start >> 4, jnp.where(row == 1, start & 15, jnp.where(row == 2, half_h, half_w))
    )
    facts = jnp.where(jnp.broadcast_to(req, (8, NR * IMG)) == me_r, facts, 0).astype(F32).astype(BF16)
    seg = ((iota((NR, NR * IMG), 1) >> 5) == iota((NR, NR * IMG), 0)).astype(BF16)
    by_src = dot_nt(facts, seg).astype(BF16)
    src_col = dot_nt(seg, facts)
    start_c = src_col[:, 0:1] * 16.0 + src_col[:, 1:2]
    off = iota((NR, L), 1).astype(F32) - start_c
    free = 1.0 - jnp.max(((off >= 0.0) & (off < float(CELLS))).astype(F32), axis=0, keepdims=True)
    earlier = (iota((L, L), 0) < iota((L, L), 1)).astype(BF16)
    rank = dot(jnp.broadcast_to(free, (8, L)).astype(BF16), earlier)[0:1, :]
    place = iota((L, L), 1)
    rest = (iota((L, L), 0).astype(F32) == jnp.where(free > 0.5, rank, -1.0)).astype(F32)

    n_col = iota((L, 1), 0) - TEXT
    n_row = iota((1, L), 1) - TEXT

    def source(n):
        e, s, c, i, j = cell_of(n)
        mag = (e + 1) >> 1
        z = (me_z + NZ + jnp.where((e & 1) == 1, mag, -mag)) & (NZ - 1)
        return jnp.where(n >= 0, 2 * z + s, -1), c, i, j

    k_col, c_c, i_c, j_c = source(n_col)
    _, c_r, i_r, j_r = source(n_row)
    expand = (k_col == iota((L, NR), 1)).astype(BF16)
    f_col = dot_nt(expand, by_src)
    f_row = dot_nt(by_src, expand)
    pos_c, valid_c = place_of(
        f_col[:, 0:1] * 16.0 + f_col[:, 1:2], f_col[:, 2:3], f_col[:, 3:4], c_c, i_c, j_c
    )
    pos_r, valid_r = place_of(
        f_row[0:1] * 16.0 + f_row[1:2], f_row[2:3], f_row[3:4], c_r, i_r, j_r
    )
    pos_c = jnp.where(n_col >= 0, pos_c, -1.0)
    to_slot[...] = (rest + (place.astype(F32) == pos_c).astype(F32)).astype(BF16)
    p8 = iota((8, L), 1)
    digits = jnp.where(iota((8, L), 0) == 0, p8 >> 4, p8 & 15).astype(F32).astype(BF16)
    rest_r = dot_nt(digits, rest.astype(BF16))
    pos_r = jnp.where(n_row >= 0, pos_r, rest_r[0:1] * 16.0 + rest_r[1:2])
    is_img_r = (n_row >= 0) & valid_r
    bad_r = ((n_row >= 0) & jnp.logical_not(valid_r)).astype(F32)

    gv2 = gv_r[...].astype(F32)
    gv = jnp.concatenate([gv2[0:1], gv2[1:2]], axis=1)
    gd2 = gd_r[...].astype(F32)
    gd_i = iota((D // HD, HD), 0)
    gd = jnp.concatenate(
        [jnp.sum(jnp.where(gd_i == 2 * me_t + h, gd2, 0.0), axis=0, keepdims=True) for h in range(2)],
        axis=1,
    )
    load_t.wait()
    xraw[...] = dot(to_slot[...], text_v[...])

    sel_r, sel_c = iota((GROUP, 4 * PACK), 0), iota((GROUP, 4 * PACK), 1)
    sel_e = (sel_r * 3641) >> 16
    sel_at = sel_e * PACK + sel_r - 18 * sel_e
    left = (sel_c == sel_at).astype(BF16)
    right = (sel_c == sel_at + 18).astype(BF16)

    def two(s, r):
        hi = s.astype(BF16).astype(F32)
        lo = s - hi

        def wide(v):
            return jnp.concatenate([v[:, W:], jnp.zeros((8, 2 * W - L), F32)], axis=1)

        return jnp.where(
            r == 0, hi[:, :W], jnp.where(r == 1, wide(hi), jnp.where(r == 2, lo[:, :W], wide(lo)))
        )

    swap = pltpu.make_async_remote_copy(
        src_ref=pool.at[:, core], dst_ref=pool.at[:, core], send_sem=p_sem.at[0],
        recv_sem=p_sem.at[1], device_id={"req": sibling}, device_id_type=MESH,
    )
    def packet(e):
        to = (me_z + shift_of(e) + NZ) & (NZ - 1)
        return pltpu.make_async_remote_copy(
            src_ref=stage.at[to], dst_ref=recv.at[mirror(e)], send_sem=a_send.at[e],
            recv_sem=a_recv.at[mirror(e)], device_id={"req": to * 2 + core}, device_id_type=MESH,
        )

    def put(x, rows):
        xfull[me_t, rows] = (x * gd).astype(BF16)
        sq_r[rows] = (x * x).astype(BF16)

    def fill(g):
        for e in range(4 * g, 4 * g + 4):
            if e:
                packet(mirror(e)).wait_recv()
        rows = slice(TEXT + GROUP * g, TEXT + GROUP * (g + 1))
        got = recv[4 * g:4 * g + 4].reshape(4 * PACK, HD)
        img = jnp.concatenate([dot(left, got), dot(right, got)], axis=1)
        x = jnp.where(valid_c[rows], img * gv, xraw[rows])
        xraw[rows] = x
        sq_i[rows] = (img * img).astype(BF16)
        put(x, rows)

    sent = []

    def x_copy(da, db, h, ka, kb, k):
        t = at(da, db)
        rows = pl.ds(*X_PARTS[h])
        return pltpu.make_async_remote_copy(
            src_ref=xfull.at[t, rows], dst_ref=xfull.at[t, rows], send_sem=x_send.at[k],
            recv_sem=x_recv.at[t, h], device_id={"tensor": at(ka, kb)}, device_id_type=MESH,
        )

    def push(da, db, h, *to):
        for ka, kb in to:
            one = x_copy(da, db, h, ka, kb, len(sent))
            one.start()
            sent.append(one)

    def wait(da, db, h):
        x_copy(da, db, h, 0, 1, 0).wait_recv()

    def w_copy(i, db):
        return pltpu.make_async_remote_copy(
            src_ref=wout_h.at[:, w_cols(at(PEERS[i], db))], dst_ref=w_blk.at[(pb + db) & 3, heads],
            send_sem=w_send.at[i, db], recv_sem=w_recv.at[i, db],
            device_id={"tensor": at(PEERS[i], 0)}, device_id_type=MESH,
        )

    def w_wait(i, db):
        rows = pl.ds(pl.multiple_of(((pa - PEERS[i]) & 3) * HD, HD), HD)
        block = w_blk.at[(pb + db) & 3, rows]
        pltpu.make_async_remote_copy(
            src_ref=block, dst_ref=block, send_sem=w_send.at[i, db], recv_sem=w_recv.at[i, db],
            device_id={"tensor": at(-PEERS[i], 0)}, device_id_type=MESH,
        ).wait_recv()

    sq_i[:TEXT] = jnp.zeros((TEXT, W), BF16)
    put(xraw[:TEXT], slice(0, TEXT))
    to_pos[...] = (iota((L, L), 0).astype(F32) == pos_r).astype(BF16)
    stat[...] = jnp.zeros_like(stat)
    acc[...] = jnp.zeros_like(acc)
    ring_b = tuple((0, d) for d in PEERS)

    pl.semaphore_wait(barrier, NZ - 1 + 1 + 2 * len(PEERS))

    swap.start()
    push(0, 0, 0, *((d, 0) for d in PEERS), *ring_b)
    for i in range(len(PEERS)):
        for db in range(4):
            w_copy(i, db).start()
    swap.wait_recv()
    stage_rows(1 - core, other)
    stage[...] = stage_f[...].astype(BF16).reshape(NZ, PACK, HD)
    for e in range(NZ - 1, 0, -1):
        packet(e).start()
    recv[0] = stage[me_z]
    for da in PEERS[::-1]:
        wait(da, 0, 0)
        push(da, 0, 0, *ring_b)

    up_a, dn_a, up_b, dn_b = (1, 0), (-1, 0), (0, 1), (0, -1)
    fill(0)
    fill(1)
    push(0, 0, 1, up_a, dn_a, up_b, dn_b)
    fill(2)
    fill(3)
    ones = jnp.ones((8, W), BF16)
    r8 = iota((8, W), 0)
    xfull[me_t, L:] = jnp.where(
        r8 < 4, two(dot_nt(ones, sq_i[...]), r8), two(dot_nt(ones, sq_r[...]), r8 - 4)
    ).astype(BF16)
    push(0, 0, 2, up_a, dn_a, up_b, dn_b)

    def project(da, db):
        if db:
            wait(da, db, 0)
        t = at(da, db)
        acc[...] += dot(xfull[t, :L], w_v[pl.ds(pl.multiple_of(t * W, W), W), :])
        stat[...] += xfull[t, L:].astype(F32)

    for one in load_w:
        one.wait()
    project(0, 0)
    wait(-1, 0, 1)
    push(-1, 0, 1, up_a, up_b, dn_b)
    wait(1, 0, 1)
    push(1, 0, 1, up_b, dn_b)
    wait(0, -1, 1)
    push(0, -1, 1, up_b)
    wait(0, 1, 1)
    wait(1, 0, 2)
    push(1, 0, 2, dn_a, up_b, dn_b)
    wait(-1, 0, 2)
    push(-1, 0, 2, up_b, dn_b)
    wait(0, 1, 2)
    push(0, 1, 2, dn_b)
    wait(0, -1, 2)
    project(1, 0)
    project(-1, 0)
    for h in (1, 2):
        wait(2, 0, h)
        push(2, 0, h, up_b, dn_b)
    for da in (-1, 1):
        wait(da, -1, 1)
        push(da, -1, 1, up_b)
        wait(da, 1, 1)
    for da in (-1, 1):
        wait(da, 1, 2)
        push(da, 1, 2, dn_b)
        wait(da, -1, 2)
    wait(0, 2, 1)
    wait(0, 2, 2)
    for one in ((0, 1), (0, -1), (2, 0), (0, 2), (1, 1), (1, -1)):
        project(*one)
    wait(2, -1, 1)
    push(2, -1, 1, up_b)
    wait(2, 1, 1)
    wait(2, 1, 2)
    push(2, 1, 2, dn_b)
    wait(2, -1, 2)
    project(-1, 1)
    project(-1, -1)
    project(2, 1)
    project(2, -1)
    for da in (-1, 1):
        wait(da, 2, 1)
        wait(da, 2, 2)
        project(da, 2)
    for one in load_o:
        one.wait()
    for i in range(len(PEERS)):
        for db in range(4):
            w_wait(i, db)
    wait(2, 2, 1)
    wait(2, 2, 2)
    project(2, 2)

    sums = stat[...]

    def whole(r):
        return jnp.concatenate(
            [sums[r:r + 1, :] + sums[r + 2:r + 3, :],
             sums[r + 1:r + 2, :L - W] + sums[r + 3:r + 4, :L - W]], axis=1
        )

    rv = jnp.where(is_img_r, lax.rsqrt(whole(0) / D + EPS), 1.0)
    rd = lax.rsqrt(rv * rv * whole(4) / D + EPS)
    cols = jnp.transpose(jnp.where(iota((8, L), 0) == 0, rv * rd, rv))
    qkv = (acc[...] * cols[:, 0:1]).astype(BF16)
    queries = dot(to_pos[...], qkv[:, :HD]).astype(BF16)

    def c_copy(b, i):
        block = ctx.at[pl.ds(*Q_PARTS[b]), heads]
        return pltpu.make_async_remote_copy(
            src_ref=block, dst_ref=block, send_sem=c_send.at[b, i], recv_sem=c_recv.at[b, i],
            device_id={"tensor": at(PEERS[i], 0)}, device_id_type=MESH,
        )

    def c_wait(b, i):
        cols = pl.ds(pl.multiple_of(((pa - PEERS[i]) & 3) * HD, HD), HD)
        block = ctx.at[pl.ds(*Q_PARTS[b]), cols]
        pltpu.make_async_remote_copy(
            src_ref=block, dst_ref=block, send_sem=c_send.at[b, i], recv_sem=c_recv.at[b, i],
            device_id={"tensor": at(-PEERS[i], 0)}, device_id_type=MESH,
        ).wait_recv()

    def o_copy(b, i):
        rows = pl.ds(*Q_PARTS[b])
        return pltpu.make_async_remote_copy(
            src_ref=part.at[i, rows], dst_ref=part_in.at[i, rows], send_sem=o_send.at[b, i],
            recv_sem=o_recv.at[b, i], device_id={"tensor": at(0, PEERS[i])}, device_id_type=MESH,
        )

    both = [(b, i) for b in range(len(Q_PARTS)) for i in range(len(PEERS))]
    for b, (lo, n) in enumerate(Q_PARTS):
        scores = dot_nt(queries[lo:lo + n], qkv[:, HD:2 * HD]) * (HD ** -0.5)
        at_q = (iota((n, L), 0) + lo).astype(F32)
        scores = jnp.where((at_q >= pos_r) & (bad_r < 0.5), scores, -1e30)
        expo = jnp.exp(scores - jnp.max(scores, axis=-1, keepdims=True))
        probs = (expo / jnp.sum(expo, axis=-1, keepdims=True)).astype(BF16)
        ctx[lo:lo + n, heads] = dot(probs, qkv[:, 2 * HD:]).astype(BF16)
        for i in range(len(PEERS)):
            c_copy(b, i).start()
    oacc[...] = dot(to_pos[...], (xraw[...] * cols[:, 1:2]).astype(BF16))
    for b, (lo, n) in enumerate(Q_PARTS):
        for i in range(len(PEERS)):
            c_wait(b, i)
        for i, db in enumerate(PEERS):
            part[i, lo:lo + n] = dot(ctx[lo:lo + n], w_blk[(pb + db) & 3]).astype(BF16)
            o_copy(b, i).start()
    for b, (lo, n) in enumerate(Q_PARTS):
        oacc[lo:lo + n] += dot(ctx[lo:lo + n], w_blk[pb])
    for b, (lo, n) in enumerate(Q_PARTS):
        total = oacc[lo:lo + n]
        for i in range(len(PEERS)):
            o_copy(b, i).wait_recv()
            total = total + part_in[i, lo:lo + n].astype(F32)
        out_r[lo:lo + n] = total.astype(BF16)

    swap.wait_send()
    for e in range(1, NZ):
        packet(e).wait_send()
    for i in range(len(PEERS)):
        for db in range(4):
            w_copy(i, db).wait_send()
    for b, i in both:
        c_copy(b, i).wait_send()
        o_copy(b, i).wait_send()
    for one in sent:
        one.wait_send()


def body(text, patches, grids, image_request, slot_start, vis_gain, dec_gain, w_qkv, w_out):
    vmem = pl.BlockSpec(memory_space=pltpu.VMEM)
    hbm = pl.BlockSpec(memory_space=pl.ANY)
    dma = pltpu.SemaphoreType.DMA
    return pl.pallas_call(
        kernel,
        out_shape=jax.ShapeDtypeStruct((L, W), BF16),
        in_specs=[hbm, hbm, vmem, vmem, vmem, vmem, vmem, hbm, hbm],
        out_specs=vmem,
        scratch_shapes=[
            pltpu.VMEM((L, W), BF16),
            pltpu.VMEM((6, 6, IMG, W), BF16),
            pltpu.VMEM((D, 3 * HD), BF16),
            pltpu.VMEM((4, 4 * HD, W), BF16),
            pltpu.VMEM((CELLS, 2, IMG, W), BF16),
            pltpu.VMEM((NZ * PACK, HD), F32),
            pltpu.VMEM((NZ, PACK, HD), BF16),
            pltpu.VMEM((NZ, PACK, HD), BF16),
            pltpu.VMEM((L, L), BF16),
            pltpu.VMEM((L, L), BF16),
            pltpu.VMEM((L, W), F32),
            pltpu.VMEM((L, W), BF16),
            pltpu.VMEM((L, W), BF16),
            pltpu.VMEM((NT, L + 8, W), BF16),
            pltpu.VMEM((L, 4 * HD), BF16),
            pltpu.VMEM((3, L, W), BF16),
            pltpu.VMEM((3, L, W), BF16),
            pltpu.VMEM((L, 3 * HD), F32),
            pltpu.VMEM((L, W), F32),
            pltpu.VMEM((8, W), F32),
            dma((9,)), dma((2,)), dma((3, 4)), dma((3, 4)), dma((NZ,)), dma((NZ,)),
            dma((48,)), dma((NT, 3)), dma((2, 3)), dma((2, 3)), dma((2, 3)), dma((2, 3)),
        ],
        compiler_params=pltpu.CompilerParams(
            collective_id=0, has_side_effects=True, vmem_limit_bytes=62 * 2**20
        ),
    )(
        text,
        patches.transpose(1, 2, 0, 3),
        grids.T,
        image_request.reshape(1, -1),
        slot_start.reshape(1, -1),
        vis_gain.reshape(-1, HD),
        dec_gain.reshape(-1, HD),
        w_qkv.transpose(1, 0, 2),
        w_out,
    )


def solution(mesh):
    in_specs = (
        P("req", "tensor"),
        P("req", None, None, "tensor"),
        P(),
        P(),
        P(),
        P("tensor"),
        P(),
        P(None, None, "tensor"),
        P("tensor", None),
    )
    return jax.shard_map(
        body, mesh=mesh, in_specs=in_specs, out_specs=P("req", "tensor"), check_vma=False
    )
```

```python
import jax
import jax.numpy as jnp
from jax import lax
from jax.experimental import pallas as pl
from jax.experimental.pallas import tpu as pltpu
from jax.sharding import PartitionSpec as P

D = 4096
HD = 128
L = 384
W = 256
NR = 32
NZ = 16
NT = 16
IMG = 32
CELLS = 9
TEXT = L - NR * CELLS
PACK = 40
GROUP = 72
EPS = 1e-05
MESH = pl.DeviceIdType.MESH
F32 = jnp.float32
BF16 = jnp.bfloat16
EARLY, SPLIT = TEXT, TEXT + 2 * GROUP
X_PARTS = ((0, EARLY), (EARLY, SPLIT - EARLY), (SPLIT, L + 8 - SPLIT))
Q_PARTS = ((0, L // 2), (L // 2, L // 2))
PEERS = (2, 1, -1)


def iota(shape, dim):
    return lax.broadcasted_iota(jnp.int32, shape, dim)


def dot(a, b):
    return lax.dot_general(a, b, (((1,), (0,)), ((), ())), preferred_element_type=F32)


def dot_nt(a, b):
    return lax.dot_general(a, b, (((1,), (1,)), ((), ())), preferred_element_type=F32)


def shift_of(e):
    return (e + 1) // 2 if e % 2 else -(e // 2)


def mirror(e):
    return e if e in (0, NZ - 1) else (e + 1 if e % 2 else e - 1)


def cell_of(n):
    e = (n * 3641) >> 16
    q = n - 18 * e
    s = (q >= CELLS).astype(jnp.int32)
    c = q - CELLS * s
    i = (c >= 3).astype(jnp.int32) + (c >= 6).astype(jnp.int32)
    return e, s, c.astype(F32), i.astype(F32), (c - 3 * i).astype(F32)


def place_of(start, hh, hw, c, i, j):
    valid = (i < hh) & (j < hw)
    before = jnp.minimum(i, hh) * hw + jnp.where(i < hh, jnp.minimum(j, hw), 0.0)
    return start + jnp.where(valid, i * hw + j, hh * hw + c - before), valid


def kernel(
    text_h, patch_h, grid_r, req_r, slot_r, gv_r, gd_r, wqkv_h, wout_h, out_r,
    text_v, patch_v, w_v, w_blk, pool, stage_f, stage, recv, to_slot, to_pos, xraw, sq_i, sq_r,
    xfull, ctx, part, part_in, acc, oacc, stat, loc_sem, p_sem, w_send, w_recv, a_send, a_recv,
    x_send, x_recv, c_send, c_recv, o_send, o_recv,
):
    me_r = lax.axis_index("req")
    me_t = lax.axis_index("tensor")
    core = me_r & 1
    me_z = me_r >> 1
    sibling = me_r + 1 - 2 * core
    tx, ty = me_t & 3, me_t >> 2
    pa, pb = tx + core * (ty - tx), ty + core * (tx - ty)
    sa, sb = 1 + 3 * core, 4 - 3 * core
    ids = {
        (da, db): ((pa + da) & 3) * sa + ((pb + db) & 3) * sb for da in range(4) for db in range(4)
    }

    def at(da, db):
        return ids[da % 4, db % 4]

    def z_peer(shift):
        return ((me_z + shift + NZ) & (NZ - 1)) * 2 + core

    def w_cols(t):
        return pl.ds(pl.multiple_of(t * W, W), W)

    heads = pl.ds(pl.multiple_of(pa * HD, HD), HD)

    load_p = pltpu.make_async_copy(patch_h, patch_v, loc_sem.at[0])
    load_t = pltpu.make_async_copy(text_h, text_v, loc_sem.at[1])
    load_w = [
        pltpu.make_async_copy(wqkv_h.at[j], w_v.at[:, pl.ds(j * HD, HD)], loc_sem.at[2 + j])
        for j in range(3)
    ]
    load_o = [
        pltpu.make_async_copy(
            wout_h.at[:, w_cols(at(0, db))], w_blk.at[(pb + db) & 3, heads], loc_sem.at[5 + db]
        )
        for db in range(4)
    ]
    load_p.start()
    barrier = pltpu.get_barrier_semaphore()

    def greet(**device):
        pl.semaphore_signal(barrier, inc=1, device_id=device, device_id_type=MESH)

    for e in range(NZ - 1, 0, -1):
        greet(req=z_peer(shift_of(e)))
    greet(req=sibling)
    for d in PEERS:
        greet(tensor=at(d, 0))
        greet(tensor=at(0, d))
    load_t.start()
    for copy in load_o + load_w:
        copy.start()

    req = req_r[...]
    req8 = jnp.broadcast_to(req.astype(F32), (8, NR * IMG)).astype(BF16)

    def pack(s):
        first = (me_z * 2 + s) * IMG
        ours = (iota((IMG, NR * IMG), 1) == first + iota((IMG, NR * IMG), 0)).astype(BF16)
        goes = dot_nt(req8, ours)[0:1, :]
        return ((iota((NZ, IMG), 0) * 2 + core).astype(F32) == goes).astype(BF16)

    def stage_rows(s, pick):
        for c in range(CELLS):
            rows = dot(pick, pool[c, s])
            stage_f[pl.ds(s * CELLS + c, NZ, stride=PACK), :] = rows[:, :HD]
            stage_f[pl.ds((2 + s) * CELLS + c, NZ, stride=PACK), :] = rows[:, HD:]

    load_p.wait()
    for c in range(CELLS):
        i, j = 2 * (c // 3), 2 * (c % 3)
        total = (
            patch_v[i, j].astype(F32) + patch_v[i, j + 1].astype(F32)
            + patch_v[i + 1, j].astype(F32) + patch_v[i + 1, j + 1].astype(F32)
        )
        pool[c, core] = (total * 0.25).astype(BF16)
    stage_f[...] = jnp.zeros_like(stage_f)

    stage_rows(core, pack(core))
    other = pack(1 - core)

    row = iota((8, NR * IMG), 0)
    start = jnp.broadcast_to(slot_r[...], (8, NR * IMG))
    half_h = jnp.broadcast_to(grid_r[0:1, :], (8, NR * IMG)) >> 1
    half_w = jnp.broadcast_to(grid_r[1:2, :], (8, NR * IMG)) >> 1
    facts = jnp.where(
        row == 0, start >> 4, jnp.where(row == 1, start & 15, jnp.where(row == 2, half_h, half_w))
    )
    facts = jnp.where(jnp.broadcast_to(req, (8, NR * IMG)) == me_r, facts, 0).astype(F32).astype(BF16)
    seg = ((iota((NR, NR * IMG), 1) >> 5) == iota((NR, NR * IMG), 0)).astype(BF16)
    by_src = dot_nt(facts, seg).astype(BF16)
    src_col = dot_nt(seg, facts)
    start_c = src_col[:, 0:1] * 16.0 + src_col[:, 1:2]
    off = iota((NR, L), 1).astype(F32) - start_c
    free = 1.0 - jnp.max(((off >= 0.0) & (off < float(CELLS))).astype(F32), axis=0, keepdims=True)
    earlier = (iota((L, L), 0) < iota((L, L), 1)).astype(BF16)
    rank = dot(jnp.broadcast_to(free, (8, L)).astype(BF16), earlier)[0:1, :]
    place = iota((L, L), 1)
    rest = (iota((L, L), 0).astype(F32) == jnp.where(free > 0.5, rank, -1.0)).astype(F32)

    n_col = iota((L, 1), 0) - TEXT
    n_row = iota((1, L), 1) - TEXT

    def source(n):
        e, s, c, i, j = cell_of(n)
        mag = (e + 1) >> 1
        z = (me_z + NZ + jnp.where((e & 1) == 1, mag, -mag)) & (NZ - 1)
        return jnp.where(n >= 0, 2 * z + s, -1), c, i, j

    k_col, c_c, i_c, j_c = source(n_col)
    _, c_r, i_r, j_r = source(n_row)
    expand = (k_col == iota((L, NR), 1)).astype(BF16)
    f_col = dot_nt(expand, by_src)
    f_row = dot_nt(by_src, expand)
    pos_c, valid_c = place_of(
        f_col[:, 0:1] * 16.0 + f_col[:, 1:2], f_col[:, 2:3], f_col[:, 3:4], c_c, i_c, j_c
    )
    pos_r, valid_r = place_of(
        f_row[0:1] * 16.0 + f_row[1:2], f_row[2:3], f_row[3:4], c_r, i_r, j_r
    )
    pos_c = jnp.where(n_col >= 0, pos_c, -1.0)
    to_slot[...] = (rest + (place.astype(F32) == pos_c).astype(F32)).astype(BF16)
    p8 = iota((8, L), 1)
    digits = jnp.where(iota((8, L), 0) == 0, p8 >> 4, p8 & 15).astype(F32).astype(BF16)
    rest_r = dot_nt(digits, rest.astype(BF16))
    pos_r = jnp.where(n_row >= 0, pos_r, rest_r[0:1] * 16.0 + rest_r[1:2])
    is_img_r = (n_row >= 0) & valid_r
    bad_r = ((n_row >= 0) & jnp.logical_not(valid_r)).astype(F32)

    gv2 = gv_r[...].astype(F32)
    gv = jnp.concatenate([gv2[0:1], gv2[1:2]], axis=1)
    gd2 = gd_r[...].astype(F32)
    gd_i = iota((D // HD, HD), 0)
    gd = jnp.concatenate(
        [jnp.sum(jnp.where(gd_i == 2 * me_t + h, gd2, 0.0), axis=0, keepdims=True) for h in range(2)],
        axis=1,
    )
    load_t.wait()
    xraw[...] = dot(to_slot[...], text_v[...])

    sel_r, sel_c = iota((GROUP, 4 * PACK), 0), iota((GROUP, 4 * PACK), 1)
    sel_e = (sel_r * 3641) >> 16
    sel_at = sel_e * PACK + sel_r - 18 * sel_e
    left = (sel_c == sel_at).astype(BF16)
    right = (sel_c == sel_at + 18).astype(BF16)

    def two(s, r):
        hi = s.astype(BF16).astype(F32)
        lo = s - hi

        def wide(v):
            return jnp.concatenate([v[:, W:], jnp.zeros((8, 2 * W - L), F32)], axis=1)

        return jnp.where(
            r == 0, hi[:, :W], jnp.where(r == 1, wide(hi), jnp.where(r == 2, lo[:, :W], wide(lo)))
        )

    swap = pltpu.make_async_remote_copy(
        src_ref=pool.at[:, core], dst_ref=pool.at[:, core], send_sem=p_sem.at[0],
        recv_sem=p_sem.at[1], device_id={"req": sibling}, device_id_type=MESH,
    )
    def packet(e):
        to = (me_z + shift_of(e) + NZ) & (NZ - 1)
        return pltpu.make_async_remote_copy(
            src_ref=stage.at[to], dst_ref=recv.at[mirror(e)], send_sem=a_send.at[e],
            recv_sem=a_recv.at[mirror(e)], device_id={"req": to * 2 + core}, device_id_type=MESH,
        )

    def put(x, rows):
        xfull[me_t, rows] = (x * gd).astype(BF16)
        sq_r[rows] = (x * x).astype(BF16)

    def fill(g):
        for e in range(4 * g, 4 * g + 4):
            if e:
                packet(mirror(e)).wait_recv()
        rows = slice(TEXT + GROUP * g, TEXT + GROUP * (g + 1))
        got = recv[4 * g:4 * g + 4].reshape(4 * PACK, HD)
        img = jnp.concatenate([dot(left, got), dot(right, got)], axis=1)
        x = jnp.where(valid_c[rows], img * gv, xraw[rows])
        xraw[rows] = x
        sq_i[rows] = (img * img).astype(BF16)
        put(x, rows)

    sent = []

    def x_copy(da, db, h, ka, kb, k):
        t = at(da, db)
        rows = pl.ds(*X_PARTS[h])
        return pltpu.make_async_remote_copy(
            src_ref=xfull.at[t, rows], dst_ref=xfull.at[t, rows], send_sem=x_send.at[k],
            recv_sem=x_recv.at[t, h], device_id={"tensor": at(ka, kb)}, device_id_type=MESH,
        )

    def push(da, db, h, *to):
        for ka, kb in to:
            one = x_copy(da, db, h, ka, kb, len(sent))
            one.start()
            sent.append(one)

    def wait(da, db, h):
        x_copy(da, db, h, 0, 1, 0).wait_recv()

    def w_copy(i, db):
        return pltpu.make_async_remote_copy(
            src_ref=wout_h.at[:, w_cols(at(PEERS[i], db))], dst_ref=w_blk.at[(pb + db) & 3, heads],
            send_sem=w_send.at[i, db], recv_sem=w_recv.at[i, db],
            device_id={"tensor": at(PEERS[i], 0)}, device_id_type=MESH,
        )

    def w_wait(i, db):
        rows = pl.ds(pl.multiple_of(((pa - PEERS[i]) & 3) * HD, HD), HD)
        block = w_blk.at[(pb + db) & 3, rows]
        pltpu.make_async_remote_copy(
            src_ref=block, dst_ref=block, send_sem=w_send.at[i, db], recv_sem=w_recv.at[i, db],
            device_id={"tensor": at(-PEERS[i], 0)}, device_id_type=MESH,
        ).wait_recv()

    sq_i[:TEXT] = jnp.zeros((TEXT, W), BF16)
    put(xraw[:TEXT], slice(0, TEXT))
    to_pos[...] = (iota((L, L), 0).astype(F32) == pos_r).astype(BF16)
    stat[...] = jnp.zeros_like(stat)
    acc[...] = jnp.zeros_like(acc)
    ring_b = tuple((0, d) for d in PEERS)

    pl.semaphore_wait(barrier, NZ - 1 + 1 + 2 * len(PEERS))

    swap.start()
    push(0, 0, 0, *((d, 0) for d in PEERS), *ring_b)
    for i in range(len(PEERS)):
        for db in range(4):
            w_copy(i, db).start()
    swap.wait_recv()
    stage_rows(1 - core, other)
    stage[...] = stage_f[:NZ * PACK].astype(BF16).reshape(NZ, PACK, HD)
    for e in range(NZ - 1, 0, -1):
        packet(e).start()
    recv[0] = stage[me_z]
    for da in PEERS[::-1]:
        wait(da, 0, 0)
        push(da, 0, 0, *ring_b)

    up_a, dn_a, up_b, dn_b = (1, 0), (-1, 0), (0, 1), (0, -1)
    fill(0)
    fill(1)
    push(0, 0, 1, up_a, dn_a, up_b, dn_b)
    fill(2)
    fill(3)
    ones = jnp.ones((8, W), BF16)
    r8 = iota((8, W), 0)
    xfull[me_t, L:] = jnp.where(
        r8 < 4, two(dot_nt(ones, sq_i[...]), r8), two(dot_nt(ones, sq_r[...]), r8 - 4)
    ).astype(BF16)
    push(0, 0, 2, up_a, dn_a, up_b, dn_b)

    def project(da, db):
        if db:
            wait(da, db, 0)
        t = at(da, db)
        acc[...] += dot(xfull[t, :L], w_v[pl.ds(pl.multiple_of(t * W, W), W), :])
        stat[...] += xfull[t, L:].astype(F32)

    for one in load_w:
        one.wait()
    project(0, 0)
    wait(-1, 0, 1)
    push(-1, 0, 1, up_a, up_b, dn_b)
    wait(1, 0, 1)
    push(1, 0, 1, up_b, dn_b)
    wait(0, -1, 1)
    push(0, -1, 1, up_b)
    wait(0, 1, 1)
    wait(1, 0, 2)
    push(1, 0, 2, dn_a, up_b, dn_b)
    wait(-1, 0, 2)
    push(-1, 0, 2, up_b, dn_b)
    wait(0, 1, 2)
    push(0, 1, 2, dn_b)
    wait(0, -1, 2)
    project(1, 0)
    project(-1, 0)
    for h in (1, 2):
        wait(2, 0, h)
        push(2, 0, h, up_b, dn_b)
    for da in (-1, 1):
        wait(da, -1, 1)
        push(da, -1, 1, up_b)
        wait(da, 1, 1)
    for da in (-1, 1):
        wait(da, 1, 2)
        push(da, 1, 2, dn_b)
        wait(da, -1, 2)
    wait(0, 2, 1)
    wait(0, 2, 2)
    for one in ((0, 1), (0, -1), (2, 0), (0, 2), (1, 1), (1, -1)):
        project(*one)
    wait(2, -1, 1)
    push(2, -1, 1, up_b)
    wait(2, 1, 1)
    wait(2, 1, 2)
    push(2, 1, 2, dn_b)
    wait(2, -1, 2)
    project(-1, 1)
    project(-1, -1)
    project(2, 1)
    project(2, -1)
    for da in (-1, 1):
        wait(da, 2, 1)
        wait(da, 2, 2)
        project(da, 2)
    for one in load_o:
        one.wait()
    for i in range(len(PEERS)):
        for db in range(4):
            w_wait(i, db)
    wait(2, 2, 1)
    wait(2, 2, 2)
    project(2, 2)

    sums = stat[...]

    def whole(r):
        return jnp.concatenate(
            [sums[r:r + 1, :] + sums[r + 2:r + 3, :],
             sums[r + 1:r + 2, :L - W] + sums[r + 3:r + 4, :L - W]], axis=1
        )

    rv = jnp.where(is_img_r, lax.rsqrt(whole(0) / D + EPS), 1.0)
    rd = lax.rsqrt(rv * rv * whole(4) / D + EPS)
    cols = jnp.transpose(jnp.where(iota((8, L), 0) == 0, rv * rd, rv))
    qkv = (acc[...] * cols[:, 0:1]).astype(BF16)
    queries = dot(to_pos[...], qkv[:, :HD]).astype(BF16)

    def c_copy(b, i):
        block = ctx.at[pl.ds(*Q_PARTS[b]), heads]
        return pltpu.make_async_remote_copy(
            src_ref=block, dst_ref=block, send_sem=c_send.at[b, i], recv_sem=c_recv.at[b, i],
            device_id={"tensor": at(PEERS[i], 0)}, device_id_type=MESH,
        )

    def c_wait(b, i):
        cols = pl.ds(pl.multiple_of(((pa - PEERS[i]) & 3) * HD, HD), HD)
        block = ctx.at[pl.ds(*Q_PARTS[b]), cols]
        pltpu.make_async_remote_copy(
            src_ref=block, dst_ref=block, send_sem=c_send.at[b, i], recv_sem=c_recv.at[b, i],
            device_id={"tensor": at(-PEERS[i], 0)}, device_id_type=MESH,
        ).wait_recv()

    def o_copy(b, i):
        rows = pl.ds(*Q_PARTS[b])
        return pltpu.make_async_remote_copy(
            src_ref=part.at[i, rows], dst_ref=part_in.at[i, rows], send_sem=o_send.at[b, i],
            recv_sem=o_recv.at[b, i], device_id={"tensor": at(0, PEERS[i])}, device_id_type=MESH,
        )

    both = [(b, i) for b in range(len(Q_PARTS)) for i in range(len(PEERS))]
    for b, (lo, n) in enumerate(Q_PARTS):
        scores = dot_nt(queries[lo:lo + n], qkv[:, HD:2 * HD]) * (HD ** -0.5)
        at_q = (iota((n, L), 0) + lo).astype(F32)
        scores = jnp.where((at_q >= pos_r) & (bad_r < 0.5), scores, -1e30)
        expo = jnp.exp(scores - jnp.max(scores, axis=-1, keepdims=True))
        probs = (expo / jnp.sum(expo, axis=-1, keepdims=True)).astype(BF16)
        ctx[lo:lo + n, heads] = dot(probs, qkv[:, 2 * HD:]).astype(BF16)
        for i in range(len(PEERS)):
            c_copy(b, i).start()
    oacc[...] = dot(to_pos[...], (xraw[...] * cols[:, 1:2]).astype(BF16))
    for b, (lo, n) in enumerate(Q_PARTS):
        for i in range(len(PEERS)):
            c_wait(b, i)
        for i, db in enumerate(PEERS):
            part[i, lo:lo + n] = dot(ctx[lo:lo + n], w_blk[(pb + db) & 3]).astype(BF16)
            o_copy(b, i).start()
    for b, (lo, n) in enumerate(Q_PARTS):
        oacc[lo:lo + n] += dot(ctx[lo:lo + n], w_blk[pb])
    for b, (lo, n) in enumerate(Q_PARTS):
        total = oacc[lo:lo + n]
        for i in range(len(PEERS)):
            o_copy(b, i).wait_recv()
            total = total + part_in[i, lo:lo + n].astype(F32)
        out_r[lo:lo + n] = total.astype(BF16)

    swap.wait_send()
    for e in range(1, NZ):
        packet(e).wait_send()
    for i in range(len(PEERS)):
        for db in range(4):
            w_copy(i, db).wait_send()
    for b, i in both:
        c_copy(b, i).wait_send()
        o_copy(b, i).wait_send()
    for one in sent:
        one.wait_send()


def body(text, patches, grids, image_request, slot_start, vis_gain, dec_gain, w_qkv, w_out):
    vmem = pl.BlockSpec(memory_space=pltpu.VMEM)
    hbm = pl.BlockSpec(memory_space=pl.ANY)
    dma = pltpu.SemaphoreType.DMA
    return pl.pallas_call(
        kernel,
        out_shape=jax.ShapeDtypeStruct((L, W), BF16),
        in_specs=[hbm, hbm, vmem, vmem, vmem, vmem, vmem, hbm, hbm],
        out_specs=vmem,
        scratch_shapes=[
            pltpu.VMEM((L, W), BF16),
            pltpu.VMEM((6, 6, IMG, W), BF16),
            pltpu.VMEM((D, 3 * HD), BF16),
            pltpu.VMEM((4, 4 * HD, W), BF16),
            pltpu.VMEM((CELLS, 2, IMG, W), BF16),
            pltpu.VMEM(((NZ + 1) * PACK, HD), F32),
            pltpu.VMEM((NZ, PACK, HD), BF16),
            pltpu.VMEM((NZ, PACK, HD), BF16),
            pltpu.VMEM((L, L), BF16),
            pltpu.VMEM((L, L), BF16),
            pltpu.VMEM((L, W), F32),
            pltpu.VMEM((L, W), BF16),
            pltpu.VMEM((L, W), BF16),
            pltpu.VMEM((NT, L + 8, W), BF16),
            pltpu.VMEM((L, 4 * HD), BF16),
            pltpu.VMEM((3, L, W), BF16),
            pltpu.VMEM((3, L, W), BF16),
            pltpu.VMEM((L, 3 * HD), F32),
            pltpu.VMEM((L, W), F32),
            pltpu.VMEM((8, W), F32),
            dma((9,)), dma((2,)), dma((3, 4)), dma((3, 4)), dma((NZ,)), dma((NZ,)),
            dma((48,)), dma((NT, 3)), dma((2, 3)), dma((2, 3)), dma((2, 3)), dma((2, 3)),
        ],
        compiler_params=pltpu.CompilerParams(
            collective_id=0, has_side_effects=True, vmem_limit_bytes=62 * 2**20
        ),
    )(
        text,
        patches.transpose(1, 2, 0, 3),
        grids.T,
        image_request.reshape(1, -1),
        slot_start.reshape(1, -1),
        vis_gain.reshape(-1, HD),
        dec_gain.reshape(-1, HD),
        w_qkv.transpose(1, 0, 2),
        w_out,
    )


def solution(mesh):
    in_specs = (
        P("req", "tensor"),
        P("req", None, None, "tensor"),
        P(),
        P(),
        P(),
        P("tensor"),
        P(),
        P(None, None, "tensor"),
        P("tensor", None),
    )
    return jax.shard_map(
        body, mesh=mesh, in_specs=in_specs, out_specs=P("req", "tensor"), check_vma=False
    )
```

```python
import jax
import jax.numpy as jnp
from jax import lax
from jax.experimental import pallas as pl
from jax.experimental.pallas import tpu as pltpu
from jax.sharding import PartitionSpec as P

D = 4096
HD = 128
L = 384
W = 256
NR = 32
NZ = 16
NT = 16
IMG = 32
CELLS = 9
TEXT = L - NR * CELLS
PACK = 40
GROUP = 72
EPS = 1e-05
MESH = pl.DeviceIdType.MESH
F32 = jnp.float32
BF16 = jnp.bfloat16
EARLY, SPLIT = TEXT, TEXT + 2 * GROUP
X_PARTS = ((0, EARLY), (EARLY, SPLIT - EARLY), (SPLIT, L + 8 - SPLIT))
Q_PARTS = ((0, 128), (128, 128), (256, 128))
PEERS = (2, 1, -1)


def iota(shape, dim):
    return lax.broadcasted_iota(jnp.int32, shape, dim)


def dot(a, b):
    return lax.dot_general(a, b, (((1,), (0,)), ((), ())), preferred_element_type=F32)


def dot_nt(a, b):
    return lax.dot_general(a, b, (((1,), (1,)), ((), ())), preferred_element_type=F32)


def shift_of(e):
    return (e + 1) // 2 if e % 2 else -(e // 2)


def mirror(e):
    return e if e in (0, NZ - 1) else (e + 1 if e % 2 else e - 1)


def cell_of(n):
    e = (n * 3641) >> 16
    q = n - 18 * e
    s = (q >= CELLS).astype(jnp.int32)
    c = q - CELLS * s
    i = (c >= 3).astype(jnp.int32) + (c >= 6).astype(jnp.int32)
    return e, s, c.astype(F32), i.astype(F32), (c - 3 * i).astype(F32)


def place_of(start, hh, hw, c, i, j):
    valid = (i < hh) & (j < hw)
    before = jnp.minimum(i, hh) * hw + jnp.where(i < hh, jnp.minimum(j, hw), 0.0)
    return start + jnp.where(valid, i * hw + j, hh * hw + c - before), valid


def kernel(
    text_h, patch_h, grid_r, req_r, slot_r, gv_r, gd_r, wqkv_h, wout_h, out_r,
    text_v, patch_v, w_v, w_blk, pool, stage_f, stage, recv, to_slot, to_pos, xraw, sq_i, sq_r,
    xfull, ctx, part, part_in, acc, oacc, stat, loc_sem, p_sem, w_send, w_recv, a_send, a_recv,
    x_send, x_recv, c_send, c_recv, o_send, o_recv,
):
    me_r = lax.axis_index("req")
    me_t = lax.axis_index("tensor")
    core = me_r & 1
    me_z = me_r >> 1
    sibling = me_r + 1 - 2 * core
    tx, ty = me_t & 3, me_t >> 2
    pa, pb = tx + core * (ty - tx), ty + core * (tx - ty)
    sa, sb = 1 + 3 * core, 4 - 3 * core
    ids = {
        (da, db): ((pa + da) & 3) * sa + ((pb + db) & 3) * sb for da in range(4) for db in range(4)
    }

    def at(da, db):
        return ids[da % 4, db % 4]

    def z_peer(shift):
        return ((me_z + shift + NZ) & (NZ - 1)) * 2 + core

    def w_cols(t):
        return pl.ds(pl.multiple_of(t * W, W), W)

    heads = pl.ds(pl.multiple_of(pa * HD, HD), HD)

    load_p = pltpu.make_async_copy(patch_h, patch_v, loc_sem.at[0])
    load_t = pltpu.make_async_copy(text_h, text_v, loc_sem.at[1])
    load_w = [
        pltpu.make_async_copy(wqkv_h.at[j], w_v.at[:, pl.ds(j * HD, HD)], loc_sem.at[2 + j])
        for j in range(3)
    ]
    load_o = [
        pltpu.make_async_copy(
            wout_h.at[:, w_cols(at(0, db))], w_blk.at[(pb + db) & 3, heads], loc_sem.at[5 + db]
        )
        for db in range(4)
    ]
    load_p.start()
    barrier = pltpu.get_barrier_semaphore()

    def greet(**device):
        pl.semaphore_signal(barrier, inc=1, device_id=device, device_id_type=MESH)

    for e in range(NZ - 1, 0, -1):
        greet(req=z_peer(shift_of(e)))
    greet(req=sibling)
    for d in PEERS:
        greet(tensor=at(d, 0))
        greet(tensor=at(0, d))
    load_t.start()
    for copy in load_o + load_w:
        copy.start()

    req = req_r[...]
    req8 = jnp.broadcast_to(req.astype(F32), (8, NR * IMG)).astype(BF16)

    def pack(s):
        first = (me_z * 2 + s) * IMG
        ours = (iota((IMG, NR * IMG), 1) == first + iota((IMG, NR * IMG), 0)).astype(BF16)
        goes = dot_nt(req8, ours)[0:1, :]
        return ((iota((NZ, IMG), 0) * 2 + core).astype(F32) == goes).astype(BF16)

    def stage_rows(s, pick):
        for c in range(CELLS):
            rows = dot(pick, pool[c, s])
            stage_f[pl.ds(s * CELLS + c, NZ, stride=PACK), :] = rows[:, :HD]
            stage_f[pl.ds((2 + s) * CELLS + c, NZ, stride=PACK), :] = rows[:, HD:]

    load_p.wait()
    for c in range(CELLS):
        i, j = 2 * (c // 3), 2 * (c % 3)
        total = (
            patch_v[i, j].astype(F32) + patch_v[i, j + 1].astype(F32)
            + patch_v[i + 1, j].astype(F32) + patch_v[i + 1, j + 1].astype(F32)
        )
        pool[c, core] = (total * 0.25).astype(BF16)
    stage_f[...] = jnp.zeros_like(stage_f)

    stage_rows(core, pack(core))
    other = pack(1 - core)

    row = iota((8, NR * IMG), 0)
    start = jnp.broadcast_to(slot_r[...], (8, NR * IMG))
    half_h = jnp.broadcast_to(grid_r[0:1, :], (8, NR * IMG)) >> 1
    half_w = jnp.broadcast_to(grid_r[1:2, :], (8, NR * IMG)) >> 1
    facts = jnp.where(
        row == 0, start >> 4, jnp.where(row == 1, start & 15, jnp.where(row == 2, half_h, half_w))
    )
    facts = jnp.where(jnp.broadcast_to(req, (8, NR * IMG)) == me_r, facts, 0).astype(F32).astype(BF16)
    seg = ((iota((NR, NR * IMG), 1) >> 5) == iota((NR, NR * IMG), 0)).astype(BF16)
    by_src = dot_nt(facts, seg).astype(BF16)
    src_col = dot_nt(seg, facts)
    start_c = src_col[:, 0:1] * 16.0 + src_col[:, 1:2]
    off = iota((NR, L), 1).astype(F32) - start_c
    free = 1.0 - jnp.max(((off >= 0.0) & (off < float(CELLS))).astype(F32), axis=0, keepdims=True)
    earlier = (iota((L, L), 0) < iota((L, L), 1)).astype(BF16)
    rank = dot(jnp.broadcast_to(free, (8, L)).astype(BF16), earlier)[0:1, :]
    place = iota((L, L), 1)
    rest = (iota((L, L), 0).astype(F32) == jnp.where(free > 0.5, rank, -1.0)).astype(F32)

    n_col = iota((L, 1), 0) - TEXT
    n_row = iota((1, L), 1) - TEXT

    def source(n):
        e, s, c, i, j = cell_of(n)
        mag = (e + 1) >> 1
        z = (me_z + NZ + jnp.where((e & 1) == 1, mag, -mag)) & (NZ - 1)
        return jnp.where(n >= 0, 2 * z + s, -1), c, i, j

    k_col, c_c, i_c, j_c = source(n_col)
    _, c_r, i_r, j_r = source(n_row)
    expand = (k_col == iota((L, NR), 1)).astype(BF16)
    f_col = dot_nt(expand, by_src)
    f_row = dot_nt(by_src, expand)
    pos_c, valid_c = place_of(
        f_col[:, 0:1] * 16.0 + f_col[:, 1:2], f_col[:, 2:3], f_col[:, 3:4], c_c, i_c, j_c
    )
    pos_r, valid_r = place_of(
        f_row[0:1] * 16.0 + f_row[1:2], f_row[2:3], f_row[3:4], c_r, i_r, j_r
    )
    pos_c = jnp.where(n_col >= 0, pos_c, -1.0)
    to_slot[...] = (rest + (place.astype(F32) == pos_c).astype(F32)).astype(BF16)
    p8 = iota((8, L), 1)
    digits = jnp.where(iota((8, L), 0) == 0, p8 >> 4, p8 & 15).astype(F32).astype(BF16)
    rest_r = dot_nt(digits, rest.astype(BF16))
    pos_r = jnp.where(n_row >= 0, pos_r, rest_r[0:1] * 16.0 + rest_r[1:2])
    is_img_r = (n_row >= 0) & valid_r
    bad_r = ((n_row >= 0) & jnp.logical_not(valid_r)).astype(F32)

    gv2 = gv_r[...].astype(F32)
    gv = jnp.concatenate([gv2[0:1], gv2[1:2]], axis=1)
    gd2 = gd_r[...].astype(F32)
    gd_i = iota((D // HD, HD), 0)
    gd = jnp.concatenate(
        [jnp.sum(jnp.where(gd_i == 2 * me_t + h, gd2, 0.0), axis=0, keepdims=True) for h in range(2)],
        axis=1,
    )
    load_t.wait()
    xraw[...] = dot(to_slot[...], text_v[...])

    sel_r, sel_c = iota((GROUP, 4 * PACK), 0), iota((GROUP, 4 * PACK), 1)
    sel_e = (sel_r * 3641) >> 16
    sel_at = sel_e * PACK + sel_r - 18 * sel_e
    left = (sel_c == sel_at).astype(BF16)
    right = (sel_c == sel_at + 18).astype(BF16)

    def two(s, r):
        hi = s.astype(BF16).astype(F32)
        lo = s - hi

        def wide(v):
            return jnp.concatenate([v[:, W:], jnp.zeros((8, 2 * W - L), F32)], axis=1)

        return jnp.where(
            r == 0, hi[:, :W], jnp.where(r == 1, wide(hi), jnp.where(r == 2, lo[:, :W], wide(lo)))
        )

    swap = pltpu.make_async_remote_copy(
        src_ref=pool.at[:, core], dst_ref=pool.at[:, core], send_sem=p_sem.at[0],
        recv_sem=p_sem.at[1], device_id={"req": sibling}, device_id_type=MESH,
    )
    def packet(e):
        to = (me_z + shift_of(e) + NZ) & (NZ - 1)
        return pltpu.make_async_remote_copy(
            src_ref=stage.at[to], dst_ref=recv.at[mirror(e)], send_sem=a_send.at[e],
            recv_sem=a_recv.at[mirror(e)], device_id={"req": to * 2 + core}, device_id_type=MESH,
        )

    def put(x, rows):
        xfull[me_t, rows] = (x * gd).astype(BF16)
        sq_r[rows] = (x * x).astype(BF16)

    def fill(g):
        for e in range(4 * g, 4 * g + 4):
            if e:
                packet(mirror(e)).wait_recv()
        rows = slice(TEXT + GROUP * g, TEXT + GROUP * (g + 1))
        got = recv[4 * g:4 * g + 4].reshape(4 * PACK, HD)
        img = jnp.concatenate([dot(left, got), dot(right, got)], axis=1)
        x = jnp.where(valid_c[rows], img * gv, xraw[rows])
        xraw[rows] = x
        sq_i[rows] = (img * img).astype(BF16)
        put(x, rows)

    sent = []

    def x_copy(da, db, h, ka, kb, k):
        t = at(da, db)
        rows = pl.ds(*X_PARTS[h])
        return pltpu.make_async_remote_copy(
            src_ref=xfull.at[t, rows], dst_ref=xfull.at[t, rows], send_sem=x_send.at[k],
            recv_sem=x_recv.at[t, h], device_id={"tensor": at(ka, kb)}, device_id_type=MESH,
        )

    def push(da, db, h, *to):
        for ka, kb in to:
            one = x_copy(da, db, h, ka, kb, len(sent))
            one.start()
            sent.append(one)

    def wait(da, db, h):
        x_copy(da, db, h, 0, 1, 0).wait_recv()

    def w_copy(i, db):
        return pltpu.make_async_remote_copy(
            src_ref=wout_h.at[:, w_cols(at(PEERS[i], db))], dst_ref=w_blk.at[(pb + db) & 3, heads],
            send_sem=w_send.at[i, db], recv_sem=w_recv.at[i, db],
            device_id={"tensor": at(PEERS[i], 0)}, device_id_type=MESH,
        )

    def w_wait(i, db):
        rows = pl.ds(pl.multiple_of(((pa - PEERS[i]) & 3) * HD, HD), HD)
        block = w_blk.at[(pb + db) & 3, rows]
        pltpu.make_async_remote_copy(
            src_ref=block, dst_ref=block, send_sem=w_send.at[i, db], recv_sem=w_recv.at[i, db],
            device_id={"tensor": at(-PEERS[i], 0)}, device_id_type=MESH,
        ).wait_recv()

    sq_i[:TEXT] = jnp.zeros((TEXT, W), BF16)
    put(xraw[:TEXT], slice(0, TEXT))
    to_pos[...] = (iota((L, L), 0).astype(F32) == pos_r).astype(BF16)
    stat[...] = jnp.zeros_like(stat)
    acc[...] = jnp.zeros_like(acc)
    ring_b = tuple((0, d) for d in PEERS)

    pl.semaphore_wait(barrier, NZ - 1 + 1 + 2 * len(PEERS))

    swap.start()
    push(0, 0, 0, *((d, 0) for d in PEERS), *ring_b)
    for i in range(len(PEERS)):
        for db in range(4):
            w_copy(i, db).start()
    swap.wait_recv()
    stage_rows(1 - core, other)
    stage[...] = stage_f[:NZ * PACK].astype(BF16).reshape(NZ, PACK, HD)
    for e in range(NZ - 1, 0, -1):
        packet(e).start()
    recv[0] = stage[me_z]
    for da in PEERS[::-1]:
        wait(da, 0, 0)
        push(da, 0, 0, *ring_b)

    up_a, dn_a, up_b, dn_b = (1, 0), (-1, 0), (0, 1), (0, -1)
    fill(0)
    fill(1)
    push(0, 0, 1, up_a, dn_a, up_b, dn_b)
    fill(2)
    fill(3)
    ones = jnp.ones((8, W), BF16)
    r8 = iota((8, W), 0)
    xfull[me_t, L:] = jnp.where(
        r8 < 4, two(dot_nt(ones, sq_i[...]), r8), two(dot_nt(ones, sq_r[...]), r8 - 4)
    ).astype(BF16)
    push(0, 0, 2, up_a, dn_a, up_b, dn_b)

    def project(da, db):
        if db:
            wait(da, db, 0)
        t = at(da, db)
        acc[...] += dot(xfull[t, :L], w_v[pl.ds(pl.multiple_of(t * W, W), W), :])
        stat[...] += xfull[t, L:].astype(F32)

    for one in load_w:
        one.wait()
    project(0, 0)
    wait(-1, 0, 1)
    push(-1, 0, 1, up_a, up_b, dn_b)
    wait(1, 0, 1)
    push(1, 0, 1, up_b, dn_b)
    wait(0, -1, 1)
    push(0, -1, 1, up_b)
    wait(0, 1, 1)
    wait(1, 0, 2)
    push(1, 0, 2, dn_a, up_b, dn_b)
    wait(-1, 0, 2)
    push(-1, 0, 2, up_b, dn_b)
    wait(0, 1, 2)
    push(0, 1, 2, dn_b)
    wait(0, -1, 2)
    for h in (1, 2):
        wait(2, 0, h)
        push(2, 0, h, up_b, dn_b)
    for da in (-1, 1):
        wait(da, -1, 1)
        push(da, -1, 1, up_b)
        wait(da, 1, 1)
    for da in (-1, 1):
        wait(da, 1, 2)
        push(da, 1, 2, dn_b)
        wait(da, -1, 2)
    for one in ((1, 0), (-1, 0), (0, 1), (0, -1)):
        project(*one)
    wait(2, -1, 1)
    push(2, -1, 1, up_b)
    wait(2, 1, 1)
    wait(2, 1, 2)
    push(2, 1, 2, dn_b)
    wait(2, -1, 2)
    wait(0, 2, 1)
    wait(0, 2, 2)
    for one in ((2, 0), (0, 2), (1, 1), (1, -1), (-1, 1), (-1, -1), (2, 1), (2, -1)):
        project(*one)
    for da in (-1, 1):
        wait(da, 2, 1)
        wait(da, 2, 2)
        project(da, 2)
    for one in load_o:
        one.wait()
    for i in range(len(PEERS)):
        for db in range(4):
            w_wait(i, db)
    wait(2, 2, 1)
    wait(2, 2, 2)
    project(2, 2)

    sums = stat[...]

    def whole(r):
        return jnp.concatenate(
            [sums[r:r + 1, :] + sums[r + 2:r + 3, :],
             sums[r + 1:r + 2, :L - W] + sums[r + 3:r + 4, :L - W]], axis=1
        )

    rv = jnp.where(is_img_r, lax.rsqrt(whole(0) / D + EPS), 1.0)
    rd = lax.rsqrt(rv * rv * whole(4) / D + EPS)
    cols = jnp.transpose(jnp.where(iota((8, L), 0) == 0, rv * rd, rv))
    qkv = (acc[...] * cols[:, 0:1]).astype(BF16)
    queries = dot(to_pos[...], qkv[:, :HD]).astype(BF16)

    def c_copy(b, i):
        block = ctx.at[pl.ds(*Q_PARTS[b]), heads]
        return pltpu.make_async_remote_copy(
            src_ref=block, dst_ref=block, send_sem=c_send.at[b, i], recv_sem=c_recv.at[b, i],
            device_id={"tensor": at(PEERS[i], 0)}, device_id_type=MESH,
        )

    def c_wait(b, i):
        cols = pl.ds(pl.multiple_of(((pa - PEERS[i]) & 3) * HD, HD), HD)
        block = ctx.at[pl.ds(*Q_PARTS[b]), cols]
        pltpu.make_async_remote_copy(
            src_ref=block, dst_ref=block, send_sem=c_send.at[b, i], recv_sem=c_recv.at[b, i],
            device_id={"tensor": at(-PEERS[i], 0)}, device_id_type=MESH,
        ).wait_recv()

    def o_copy(b, i):
        rows = pl.ds(*Q_PARTS[b])
        return pltpu.make_async_remote_copy(
            src_ref=part.at[i, rows], dst_ref=part_in.at[i, rows], send_sem=o_send.at[b, i],
            recv_sem=o_recv.at[b, i], device_id={"tensor": at(0, PEERS[i])}, device_id_type=MESH,
        )

    both = [(b, i) for b in range(len(Q_PARTS)) for i in range(len(PEERS))]
    for b, (lo, n) in enumerate(Q_PARTS):
        scores = dot_nt(queries[lo:lo + n], qkv[:, HD:2 * HD]) * (HD ** -0.5)
        at_q = (iota((n, L), 0) + lo).astype(F32)
        scores = jnp.where((at_q >= pos_r) & (bad_r < 0.5), scores, -1e30)
        expo = jnp.exp(scores - jnp.max(scores, axis=-1, keepdims=True))
        probs = (expo / jnp.sum(expo, axis=-1, keepdims=True)).astype(BF16)
        ctx[lo:lo + n, heads] = dot(probs, qkv[:, 2 * HD:]).astype(BF16)
        for i in range(len(PEERS)):
            c_copy(b, i).start()
    oacc[...] = dot(to_pos[...], (xraw[...] * cols[:, 1:2]).astype(BF16))
    for b, (lo, n) in enumerate(Q_PARTS):
        for i in range(len(PEERS)):
            c_wait(b, i)
        for i, db in enumerate(PEERS):
            part[i, lo:lo + n] = dot(ctx[lo:lo + n], w_blk[(pb + db) & 3]).astype(BF16)
            o_copy(b, i).start()
    for b, (lo, n) in enumerate(Q_PARTS):
        oacc[lo:lo + n] += dot(ctx[lo:lo + n], w_blk[pb])
    for b, (lo, n) in enumerate(Q_PARTS):
        total = oacc[lo:lo + n]
        for i in range(len(PEERS)):
            o_copy(b, i).wait_recv()
            total = total + part_in[i, lo:lo + n].astype(F32)
        out_r[lo:lo + n] = total.astype(BF16)

    swap.wait_send()
    for e in range(1, NZ):
        packet(e).wait_send()
    for i in range(len(PEERS)):
        for db in range(4):
            w_copy(i, db).wait_send()
    for b, i in both:
        c_copy(b, i).wait_send()
        o_copy(b, i).wait_send()
    for one in sent:
        one.wait_send()


def body(text, patches, grids, image_request, slot_start, vis_gain, dec_gain, w_qkv, w_out):
    vmem = pl.BlockSpec(memory_space=pltpu.VMEM)
    hbm = pl.BlockSpec(memory_space=pl.ANY)
    dma = pltpu.SemaphoreType.DMA
    return pl.pallas_call(
        kernel,
        out_shape=jax.ShapeDtypeStruct((L, W), BF16),
        in_specs=[hbm, hbm, vmem, vmem, vmem, vmem, vmem, hbm, hbm],
        out_specs=vmem,
        scratch_shapes=[
            pltpu.VMEM((L, W), BF16),
            pltpu.VMEM((6, 6, IMG, W), BF16),
            pltpu.VMEM((D, 3 * HD), BF16),
            pltpu.VMEM((4, 4 * HD, W), BF16),
            pltpu.VMEM((CELLS, 2, IMG, W), BF16),
            pltpu.VMEM(((NZ + 1) * PACK, HD), F32),
            pltpu.VMEM((NZ, PACK, HD), BF16),
            pltpu.VMEM((NZ, PACK, HD), BF16),
            pltpu.VMEM((L, L), BF16),
            pltpu.VMEM((L, L), BF16),
            pltpu.VMEM((L, W), F32),
            pltpu.VMEM((L, W), BF16),
            pltpu.VMEM((L, W), BF16),
            pltpu.VMEM((NT, L + 8, W), BF16),
            pltpu.VMEM((L, 4 * HD), BF16),
            pltpu.VMEM((3, L, W), BF16),
            pltpu.VMEM((3, L, W), BF16),
            pltpu.VMEM((L, 3 * HD), F32),
            pltpu.VMEM((L, W), F32),
            pltpu.VMEM((8, W), F32),
            dma((9,)), dma((2,)), dma((3, 4)), dma((3, 4)), dma((NZ,)), dma((NZ,)),
            dma((48,)), dma((NT, 3)), dma((3, 3)), dma((3, 3)), dma((3, 3)), dma((3, 3)),
        ],
        compiler_params=pltpu.CompilerParams(
            collective_id=0, has_side_effects=True, vmem_limit_bytes=62 * 2**20
        ),
    )(
        text,
        patches.transpose(1, 2, 0, 3),
        grids.T,
        image_request.reshape(1, -1),
        slot_start.reshape(1, -1),
        vis_gain.reshape(-1, HD),
        dec_gain.reshape(-1, HD),
        w_qkv.transpose(1, 0, 2),
        w_out,
    )


def solution(mesh):
    in_specs = (
        P("req", "tensor"),
        P("req", None, None, "tensor"),
        P(),
        P(),
        P(),
        P("tensor"),
        P(),
        P(None, None, "tensor"),
        P("tensor", None),
    )
    return jax.shard_map(
        body, mesh=mesh, in_specs=in_specs, out_specs=P("req", "tensor"), check_vma=False
    )
```
